32 devices in a mesh: ex: 4 (over z), col: 4 (over y, core), lay: 2 (over x).
Axes of the slice: x: 2, y: 2, z: 4, core: 2. Of those that a mesh axis runs over, the one named last changes fastest.
Arguments:
- normalized: bfloat16 [256, 2, 4, 3584], P('ex', 'lay', None, 'col'), may hold values from -6 to 6
- upstream: bfloat16 [256, 2, 4, 3584], P('ex', 'lay', None, 'col'), may hold values from -3 to 3
- owner_order: int32 [4, 64], P('ex'), may hold values from 0 to 63, each once within a row
- sketch_index: int32 [2, 28, 4], P(None, 'col'), may hold values from 0 to 63, all different within a row
- sketch_scale: bfloat16 [2, 28, 4], P(None, 'col'), may hold values from -1.5 to 1.5
- query_sketch: bfloat16 [4, 8192], P('ex', 'col'), may hold values from -0.0625 to 0.0625
Outputs:
- sketch: bfloat16 [256, 8192], P(('ex', 'lay'), 'col')
- scores: float32 [256, 4], P(('ex', 'lay'), 'col')
The draws below stay inside these ranges and needn't reach their ends.
Inputs may be any that keep to these rules, and one draw needn't show every extreme that they name: Each row is an ordering of the 64 examples of one block; the example at place j of row g is training example g * 64 + owner_order[g, j]. `sketch_index`: the 4 output blocks of one input block are distinct; every output block is named by some input block.
All inputs are finite; a program needn't handle non-finite values.
Results may differ from the reference program's by a relative error of at most 0.0049.
Values may be sent and summed in bfloat16 or wider, within the bound.
A program may use at most 64 MiB of HBM per device.

```python
import math
import jax
import jax.numpy as jnp
from jax import lax

D = 3584
SKETCH = 8192
KS = 4
T_EX = 4
EX_DEV = 64
EXAMPLES = 256
LAYERS = 2
QUERIES = 4
GROUPS = 4
DB = 28
NB = 64


def levels(stream_key, dims, shards, low, top_value):
    def one(position, parts):
        draws = jax.random.uniform(jax.random.fold_in(jax.random.fold_in(stream_key, 6), position), (parts,), jnp.float32, low / len(shards), top_value / len(shards))
        return jnp.repeat(jnp.exp(draws), dims[position] // parts).reshape((-1,) + (1,) * (len(dims) - position - 1))

    gain = one(*shards[0])
    for cut in shards[1:]:
        gain = gain * one(*cut)
    return gain


def different_ones(stream_key, rows, number_of, top, lift):
    order = jax.random.permutation(jax.random.fold_in(stream_key, 1), number_of)
    boost = order
    for power in range(3):
        boost = boost * boost // number_of
    boost = boost * lift // number_of
    chance = jax.random.randint(jax.random.fold_in(stream_key, 2), (rows, number_of), 0, 4096) + boost
    holders = jax.random.permutation(jax.random.fold_in(stream_key, 3), rows)[jnp.arange(number_of) % rows]
    chance = jnp.where(jnp.arange(rows)[:, None] == holders[None, :], 1 << 14, chance)
    merit = chance * number_of + jnp.arange(number_of)
    return lax.top_k(merit.astype(jnp.int32), top)[1].astype(jnp.int32)


def normal_values(own_key, dims, width, limit, cuts=(), kind=jnp.bfloat16):
    loudness = levels(own_key, dims, cuts, -0.22, 0.18) if cuts else 1.0
    drawn = jax.random.normal(own_key, dims, jnp.float32) * width * loudness
    return jnp.minimum(jnp.maximum(drawn, -limit), limit).astype(kind)


def setup_inputs(seed: int = 0) -> dict:
    keys = jax.random.split(jax.random.key(seed), 7)
    return {
        "normalized": normal_values(keys[0], (EXAMPLES, LAYERS, T_EX, D), 1.0, 6.0, ((0, 4), (1, 2), (3, 4))),
        "upstream": normal_values(keys[1], (EXAMPLES, LAYERS, T_EX, D), 0.35, 3.0, ((0, 4), (1, 2), (3, 4))),
        "owner_order": jax.vmap(lambda own: jax.random.permutation(own, EX_DEV))(jax.random.split(keys[2], GROUPS)).reshape((GROUPS, EX_DEV)).astype(jnp.int32),
        "sketch_index": different_ones(keys[3], LAYERS * DB, NB, KS, 0).reshape((LAYERS, DB, KS)),
        "sketch_scale": normal_values(keys[4], (LAYERS, DB, KS), 0.25, 1.5, ((1, 4),)),
        "query_sketch": normal_values(keys[5], (QUERIES, SKETCH), SKETCH ** -0.5, 0.0625, ((0, 4), (1, 4))),
    }


def hadamard_table():
    counter = jnp.arange(128, dtype=jnp.int32)
    both = counter[:, None] & counter[None, :]
    parity = jnp.zeros((128, 128), jnp.int32)
    for shift_bit in range(7):
        parity = parity + (both >> shift_bit & 1)
    signs = 1 - 2 * (parity % 2)
    return signs.astype(jnp.float32) / math.sqrt(128.0)

def reference(normalized, upstream, owner_order, sketch_index, sketch_scale, query_sketch):

    def layer_grad(layer):
        left = lax.dynamic_index_in_dim(normalized, layer, 1, keepdims=False).astype(jnp.float32)
        right = lax.dynamic_index_in_dim(upstream, layer, 1, keepdims=False).astype(jnp.float32)
        return lax.optimization_barrier(jnp.sum(left * right, axis=1)).astype(jnp.bfloat16)
    per_layer = lax.map(layer_grad, jnp.arange(LAYERS, dtype=jnp.int32))
    grads = jnp.transpose(per_layer, (1, 0, 2))
    positions = jnp.arange(EXAMPLES, dtype=jnp.int32)
    order = positions // EX_DEV * EX_DEV + owner_order.reshape(-1).astype(jnp.int32)
    ordered = jnp.take(grads, order, axis=0)
    targets = jnp.arange(NB, dtype=jnp.int32)
    table = (sketch_index[..., None] == targets).astype(jnp.float32) * sketch_scale.astype(jnp.float32)[..., None]
    table = lax.optimization_barrier(jnp.sum(table, axis=2)).reshape(LAYERS * DB, NB)
    rows = ordered.reshape(EXAMPLES, LAYERS * DB, 128).astype(jnp.float32)
    mixed = jnp.einsum('ebc,bo->eoc', rows, table, precision=lax.Precision.HIGHEST)
    rotated = jnp.einsum('eoc,cd->eod', mixed, hadamard_table(), precision=lax.Precision.HIGHEST)
    sketch = rotated.reshape(EXAMPLES, SKETCH).astype(jnp.bfloat16)
    scores = jnp.einsum('ec,qc->eq', sketch.astype(jnp.float32), query_sketch.astype(jnp.float32), precision=lax.Precision.HIGHEST)
    return (sketch, scores)
```

```python
import functools
import math

import jax
import jax.numpy as jnp
from jax import lax
from jax.experimental import pallas as pl
from jax.experimental.pallas import tpu as pltpu
from jax.sharding import PartitionSpec as P

MESH = pl.DeviceIdType.MESH
LANES = 128
WAVES = 4
GROUP = 4
TILE = 16


def cuts(total):
    waves = min(WAVES, total)
    sizes = [total // waves + (i < total % waves) for i in range(waves)]
    return [(sum(sizes[:i]), sizes[i]) for i in range(waves)]


def signs():
    bits = lax.broadcasted_iota(jnp.int32, (LANES, LANES), 0) & lax.broadcasted_iota(
        jnp.int32, (LANES, LANES), 1
    )
    bits = bits ^ (bits >> 4)
    bits = bits ^ (bits >> 2)
    bits = bits ^ (bits >> 1)
    return (1 - 2 * (bits & 1)).astype(jnp.float32).astype(jnp.bfloat16)


def kernel(
    sizes,
    x_hbm,
    u_hbm,
    order_hbm,
    index_hbm,
    scale_hbm,
    query_hbm,
    sketch_ref,
    scores_ref,
    order_ref,
    index_ref,
    scale_ref,
    query_ref,
    xu_ref,
    owned_ref,
    arrived_ref,
    sibling_ref,
    own_tab_ref,
    tabs_ref,
    own_query_f32_ref,
    own_query_ref,
    queries_ref,
    had_ref,
    splat_ref,
    turned_tab_ref,
    weights_ref,
    rot_ref,
    total_ref,
    score_ref,
    load_sem,
    small_sem,
    send_sem,
    wave_sem,
    sibling_sem,
    tab_sem,
    query_sem,
    ready_sem,
):
    n_ex, n_col, n_lay, per_col, k_sel = sizes
    ex, col, lay = lax.axis_index("ex"), lax.axis_index("col"), lax.axis_index("lay")
    examples, tokens, features = x_hbm.shape
    pack = TILE // tokens
    rows = examples // n_lay
    in_blocks = features // LANES
    layers = index_ref.shape[0]
    stride = LANES // layers
    out_blocks = query_ref.shape[1] // LANES
    half = n_col // 2
    others = n_lay * half - 1
    core, chip = lax.rem(col, 2), lay * half + col // 2
    sibling = col + 1 - 2 * core
    scale = 1.0 / math.sqrt(float(LANES))
    waves = cuts(in_blocks)

    load_parts = [pl.ds(0, waves[0][1] * LANES)]
    if len(waves) > 1:
        load_parts.append(pl.ds(waves[1][0] * LANES, features - waves[1][0] * LANES))
    smalls = [
        pltpu.make_async_copy(source, held, small_sem.at[i])
        for i, (source, held) in enumerate(
            [
                (order_hbm, order_ref),
                (index_hbm, index_ref),
                (scale_hbm, scale_ref),
                (query_hbm, query_ref),
            ]
        )
    ]
    smalls[0].start()
    for k, part in enumerate(load_parts):
        for i, source in enumerate((x_hbm, u_hbm)):
            split = source.reshape(examples // pack, pack, tokens, features)
            for r in range(pack):
                pltpu.make_async_copy(
                    split.at[:, r, :, part],
                    xu_ref.at[i, :, pl.ds(r * tokens, tokens), part],
                    load_sem.at[k],
                ).start()
        if k == 0:
            for copy in smalls[1:]:
                copy.start()

    barrier = pltpu.get_barrier_semaphore()
    asker = ex // per_col
    asked_first = col * per_col

    def greet(sem, at_ex, at_col, at_lay):
        pl.semaphore_signal(
            sem,
            inc=1,
            device_id={"ex": at_ex, "col": at_col, "lay": at_lay},
            device_id_type=MESH,
        )

    for dl in reversed(range(n_lay)):
        for dc in reversed(range(n_col)):
            if dl or dc:
                greet(barrier, ex, lax.rem(col + dc, n_col), lax.rem(lay + dl, n_lay))

    def greet_askers(at_ex, carry):
        greet(barrier, at_ex, asker, lay)
        return carry

    def greet_sources(sem):
        def body(at_ex, carry):
            for at_col in range(n_col):
                greet(sem, at_ex, at_col, lay)
            return carry

        return body

    lax.fori_loop(ex + 1, n_ex, greet_askers, 0)
    lax.fori_loop(
        jnp.maximum(ex + 1, asked_first), asked_first + per_col, greet_sources(barrier), 0
    )
    below = jnp.clip(ex - asked_first, 0, per_col)
    greetings = n_lay * n_col - 1 + ex + n_col * below

    had_ref[...] = signs()
    own_tab_ref[...] = jnp.full(own_tab_ref.shape, -1.0, jnp.float32)

    def turn(stacked):
        return jnp.dot(stacked, had_ref[...], preferred_element_type=jnp.float32)

    def wave_part(k):
        first, count = waves[k]
        return pl.ds(2 * others * first, 2 * others * count)

    def piece_copy(k, number):
        first, count = waves[k]
        target = number + (chip <= number).astype(jnp.int32)
        slot = chip - (chip > target).astype(jnp.int32)
        to_lay = target // half
        return pltpu.make_async_remote_copy(
            src_ref=owned_ref.at[to_lay, pl.ds(first, count)],
            dst_ref=arrived_ref.at[
                pl.ds(2 * others * first + (2 * slot + core) * count, count)
            ],
            send_sem=send_sem.at[0],
            recv_sem=wave_sem.at[k],
            device_id={"ex": ex, "col": 2 * lax.rem(target, half) + 1, "lay": to_lay},
            device_id_type=MESH,
        )

    def to_sibling(source, target, send, recv):
        return pltpu.make_async_remote_copy(
            src_ref=source,
            dst_ref=target,
            send_sem=send,
            recv_sem=recv,
            device_id={"ex": ex, "col": sibling, "lay": lay},
            device_id_type=MESH,
        )

    def own_copy(first, count):
        part = pl.ds(first, count)
        return to_sibling(
            owned_ref.at[lay, part], sibling_ref.at[part], send_sem.at[1], sibling_sem.at[0]
        )

    def relay_copy(k):
        part = arrived_ref.at[wave_part(k)]
        return to_sibling(part, part, send_sem.at[2], wave_sem.at[k])

    def tab_copy(dc):
        return pltpu.make_async_remote_copy(
            src_ref=tabs_ref.at[0],
            dst_ref=tabs_ref.at[dc],
            send_sem=tab_sem.at[0],
            recv_sem=tab_sem.at[1],
            device_id={"ex": ex, "col": lax.rem(col + dc, n_col), "lay": lay},
            device_id_type=MESH,
        )

    def all_tabs():
        part = tabs_ref.at[pl.ds(1, n_col - 1)]
        return to_sibling(part, part, tab_sem.at[0], tab_sem.at[1])

    smalls[0].wait()
    chosen = (
        lax.broadcasted_iota(jnp.int32, (examples * tokens, examples), 0) // tokens
        == order_ref[...]
    ).astype(jnp.float32)
    chosen = chosen.T.astype(jnp.bfloat16)
    for copy in smalls[1:]:
        copy.wait()
    for layer in range(layers):
        at = slice(stride * layer, stride * layer + in_blocks)
        own_tab_ref[0:k_sel, at] = index_ref[layer].astype(jnp.float32)
        own_tab_ref[k_sel : 2 * k_sel, at] = scale_ref[layer].astype(jnp.float32)
    tabs_ref[0] = own_tab_ref[...].astype(jnp.bfloat16)
    for o in range(out_blocks):
        own_query_f32_ref[o : o + 1, :] = query_ref[:, o * LANES : (o + 1) * LANES].astype(
            jnp.float32
        )
    own_query_ref[...] = own_query_f32_ref[...].astype(jnp.bfloat16)

    for k, (first, count) in enumerate(waves):
        if k < len(load_parts):
            part = load_parts[k]
            pltpu.make_async_copy(
                xu_ref.at[:, :, :, part], xu_ref.at[:, :, :, part], load_sem.at[k]
            ).wait()
        x, u = (
            xu_ref[i, :, :, first * LANES : (first + count) * LANES]
            .reshape(examples * tokens, count * LANES)
            .astype(jnp.float32)
            for i in range(2)
        )
        product = x * u
        high = product.astype(jnp.bfloat16)
        low = (product - high.astype(jnp.float32)).astype(jnp.bfloat16)
        ordered = (
            jnp.dot(chosen, high, preferred_element_type=jnp.float32)
            + jnp.dot(chosen, low, preferred_element_type=jnp.float32)
        ).astype(jnp.bfloat16)
        stacked = jnp.concatenate(
            [ordered[:, b * LANES : (b + 1) * LANES] for b in range(count)], axis=0
        )
        if k:
            stacked = turn(stacked).astype(jnp.bfloat16)
        for owner in range(n_lay):
            for b in range(count):
                at = b * examples + owner * rows
                owned_ref[owner, first + b] = stacked[at : at + rows]
        if k == 0:
            pl.semaphore_wait(barrier, greetings)
            lax.fori_loop(
                asked_first,
                jnp.minimum(asked_first + per_col, ex),
                greet_sources(ready_sem.at[0]),
                0,
            )
        if others:
            piece_copy(k, 0).start()
        if k == 0:
            for dc in range(1, n_col):
                tab_copy(dc).start()
        else:
            for number in range(1, others):
                piece_copy(k - 1, number).start()
        own_copy(first, count).start()
    for number in range(1, others):
        piece_copy(len(waves) - 1, number).start()

    place = lax.rem(ex, per_col) * n_col + col
    mine = asker == col

    def query_copy(target):
        return pltpu.make_async_remote_copy(
            src_ref=own_query_ref,
            dst_ref=queries_ref.at[place],
            send_sem=query_sem.at[0],
            recv_sem=query_sem.at[1],
            device_id={"ex": target, "col": asker, "lay": lay},
            device_id_type=MESH,
        )

    def send_query(target, carry):
        query_copy(target).start()
        return carry

    @pl.when(mine)
    def _():
        pltpu.make_async_copy(own_query_ref, queries_ref.at[place], query_sem.at[1]).start()

    pl.when(jnp.logical_not(mine))(lambda: query_copy(ex).start())
    lax.fori_loop(0, ex, send_query, 0)

    def queries_up():
        @pl.when(ex < n_ex - 1)
        def _():
            pl.semaphore_wait(ready_sem.at[0], n_ex - 1 - ex)
            lax.fori_loop(ex + 1, n_ex, send_query, 0)

    def slot_of(source):
        return lax.rem(col - source + n_col, n_col)

    def table(slot, first, count):
        tab = tabs_ref[slot].astype(jnp.float32)
        targets = (first + lax.broadcasted_iota(jnp.int32, (count, LANES), 0)).astype(jnp.float32)
        value = jnp.zeros((count, LANES), jnp.float32)
        for k in range(k_sel):
            value = value + jnp.where(
                targets == tab[k : k + 1, :], tab[k_sel + k : k_sel + k + 1, :], 0.0
            )
        return value

    def spread(slot):
        own = table(slot, col * out_blocks, out_blocks) * scale
        for at_lay in range(layers):
            for b in range(in_blocks):
                at = stride * at_lay + b
                splat_ref[at_lay, slot, b] = jnp.broadcast_to(
                    own[:, at : at + 1], (out_blocks, LANES)
                )

    metas = []

    def combine(source, blocks, turned, first=False, last=False):
        base, count = len(metas), len(blocks)
        metas.extend(blocks)
        if turned:
            rot_ref[base : base + count] = source.astype(jnp.float32)
        else:
            rot_ref[base : base + count] = turn(source.reshape(count * rows, LANES)).reshape(
                count, rows, LANES
            )
        for o in range(0, out_blocks, GROUP):
            if first:
                sums = [jnp.zeros((rows, LANES), jnp.float32) for _ in range(GROUP)]
            else:
                sums = [total_ref[o + g] for g in range(GROUP)]
            for i, (at_lay, slot, b) in enumerate(blocks):
                value = rot_ref[base + i]
                for g in range(GROUP):
                    sums[g] = sums[g] + value * splat_ref[at_lay, slot, b, o + g : o + g + 1, :]
            for g in range(GROUP):
                if last:
                    sketch_ref[:, (o + g) * LANES : (o + g + 1) * LANES] = sums[g].astype(
                        jnp.bfloat16
                    )
                else:
                    total_ref[o + g] = sums[g]

    def await_wave(k):
        part = arrived_ref.at[wave_part(k)]
        to_sibling(part, part, send_sem.at[2], wave_sem.at[k]).wait_recv()

    def combine_wave(k, last=False):
        first, count = waves[k]
        blocks = []
        for number in range(others):
            source = number + (chip <= number).astype(jnp.int32)
            for odd in range(2):
                slot = slot_of(2 * lax.rem(source, half) + odd)
                blocks += [(source // half, slot, first + b) for b in range(count)]
        low = 2 * others * first
        combine(arrived_ref[low : low + 2 * others * count], blocks, k > 0, last=last)
        add_scores(len(metas) - len(blocks), len(metas))

    early = waves[0][1]
    spread(0)
    combine(owned_ref[lay, :early], [(lay, 0, b) for b in range(early)], False, first=True)
    combine(owned_ref[lay, early:], [(lay, 0, b) for b in range(early, in_blocks)], True)

    all_tabs().wait_recv()
    for slot in range(1, n_col):
        spread(slot)
    to_sibling(sibling_ref, sibling_ref, send_sem.at[1], sibling_sem.at[0]).wait_recv()
    near = slot_of(sibling)
    combine(sibling_ref[:early], [(lay, near, b) for b in range(early)], False)
    combine(sibling_ref[early:], [(lay, near, b) for b in range(early, in_blocks)], True)
    for slot in range(n_col):
        whole = table(slot, 0, n_col * out_blocks).T
        turned_tab_ref[slot] = whole.astype(jnp.bfloat16)

    def add_scores(start, stop):
        for q in range(per_col):
            value = score_ref[q]
            for i in range(start, stop):
                at_lay, slot, b = metas[i]
                value = value + rot_ref[i] * weights_ref[
                    slot, at_lay, b : b + 1, q * LANES : (q + 1) * LANES
                ]
            score_ref[q] = value

    def start_scores(stop):
        pltpu.make_async_copy(queries_ref, queries_ref, query_sem.at[1]).wait()
        asked = jnp.concatenate(
            [
                queries_ref[j * n_col : (j + 1) * n_col]
                .astype(jnp.float32)
                .reshape(n_col * out_blocks, LANES)
                for j in range(per_col)
            ],
            axis=1,
        ).astype(jnp.bfloat16)
        weights_ref[...] = jnp.dot(
            turned_tab_ref[...].reshape(n_col * LANES, n_col * out_blocks),
            asked,
            preferred_element_type=jnp.float32,
        ).reshape(weights_ref.shape)
        score_ref[...] = jnp.zeros_like(score_ref)
        add_scores(0, stop)

    timely = jnp.logical_and(asked_first == ex, per_col == 1)

    @pl.when(timely)
    def _():
        start_scores(2 * in_blocks)

    @pl.when(jnp.logical_not(timely))
    def _():
        weights_ref[...] = jnp.zeros_like(weights_ref)
        score_ref[...] = jnp.zeros_like(score_ref)

    odd_core = core == 1
    pl.when(jnp.logical_not(odd_core))(queries_up)
    last = len(waves) - 1
    for k in range(len(waves)):
        await_wave(k)
        pl.when(odd_core)(lambda: relay_copy(k).start())
        combine_wave(k, last=k == last)
        if k == 0:
            pl.when(odd_core)(queries_up)

    pl.when(jnp.logical_not(timely))(lambda: start_scores(len(metas)))
    for q in range(per_col):
        scores_ref[q : q + 1, :] = jnp.sum(score_ref[q].T, axis=0, keepdims=True) * scale

    part = arrived_ref.at[pl.ds(0, others * in_blocks)]
    to_sibling(part, part, send_sem.at[0], wave_sem.at[0]).wait_send()
    to_sibling(sibling_ref, sibling_ref, send_sem.at[1], sibling_sem.at[0]).wait_send()
    all_tabs().wait_send()

    @pl.when(odd_core)
    def _():
        to_sibling(arrived_ref, arrived_ref, send_sem.at[2], wave_sem.at[0]).wait_send()

    def sent_queries(count):
        part = queries_ref.at[pl.ds(0, count)]
        to_sibling(part, part, query_sem.at[0], query_sem.at[1]).wait_send()

    pl.when(jnp.logical_not(mine))(lambda: sent_queries(n_ex))
    if n_ex > 1:
        pl.when(mine)(lambda: sent_queries(n_ex - 1))


def put_out(sketch_ref, scores_ref, sketch_hbm, scores_hbm, sem):
    copies = [
        pltpu.make_async_copy(sketch_ref, sketch_hbm, sem.at[0]),
        pltpu.make_async_copy(scores_ref, scores_hbm, sem.at[1]),
    ]
    for copy in copies:
        copy.start()
    for copy in copies:
        copy.wait()


def solution(mesh):
    n_ex, n_col, n_lay = (mesh.shape[name] for name in ("ex", "col", "lay"))

    def local(normalized, upstream, owner_order, sketch_index, sketch_scale, query_sketch):
        examples, own_layers, tokens, features = normalized.shape
        layers, in_blocks, k_sel = sketch_index.shape
        width = query_sketch.shape[1]
        out_blocks = width // LANES
        assert TILE % tokens == 0 and examples * tokens % TILE == 0
        assert own_layers == 1 and query_sketch.shape[0] == 1 and n_col % 2 == 0
        assert n_col * out_blocks <= 256 and in_blocks <= LANES // layers
        per_col = n_ex // n_col
        rows = examples // n_lay
        waves = len(cuts(in_blocks))
        others = n_lay * n_col // 2 - 1
        vmem = pl.BlockSpec(memory_space=pltpu.VMEM)
        hbm = pl.BlockSpec(memory_space=pl.ANY)
        dma = pltpu.SemaphoreType.DMA
        sketch, scores = pl.pallas_call(
            functools.partial(kernel, (n_ex, n_col, n_lay, per_col, k_sel)),
            out_shape=(
                pltpu.VMEM((rows, width), jnp.bfloat16),
                pltpu.VMEM((per_col, rows), jnp.float32),
            ),
            in_specs=[hbm] * 6,
            out_specs=(vmem, vmem),
            scratch_shapes=[
                pltpu.VMEM(owner_order.shape, jnp.int32),
                pltpu.VMEM((layers, k_sel, in_blocks), jnp.int32),
                pltpu.VMEM((layers, k_sel, in_blocks), jnp.bfloat16),
                pltpu.VMEM(query_sketch.shape, jnp.bfloat16),
                pltpu.VMEM((2, examples * tokens // TILE, TILE, features), jnp.bfloat16),
                pltpu.VMEM((n_lay, in_blocks, rows, LANES), jnp.bfloat16),
                pltpu.VMEM((2 * others * in_blocks, rows, LANES), jnp.bfloat16),
                pltpu.VMEM((in_blocks, rows, LANES), jnp.bfloat16),
                pltpu.VMEM((2 * k_sel, LANES), jnp.float32),
                pltpu.VMEM((n_col, 2 * k_sel, LANES), jnp.bfloat16),
                pltpu.VMEM((out_blocks, LANES), jnp.float32),
                pltpu.VMEM((out_blocks, LANES), jnp.bfloat16),
                pltpu.VMEM((n_ex, out_blocks, LANES), jnp.bfloat16),
                pltpu.VMEM((LANES, LANES), jnp.bfloat16),
                pltpu.VMEM((layers, n_col, in_blocks, out_blocks, LANES), jnp.float32),
                pltpu.VMEM((n_col, LANES, n_col * out_blocks), jnp.bfloat16),
                pltpu.VMEM((n_col, layers, LANES // layers, per_col * LANES), jnp.float32),
                pltpu.VMEM((n_lay * n_col * in_blocks, rows, LANES), jnp.float32),
                pltpu.VMEM((out_blocks, rows, LANES), jnp.float32),
                pltpu.VMEM((per_col, rows, LANES), jnp.float32),
                dma((min(waves, 2),)),
                dma((4,)),
                dma((3,)),
                dma((waves,)),
                dma((1,)),
                dma((2,)),
                dma((2,)),
                pltpu.SemaphoreType.REGULAR((1,)),
            ],
            compiler_params=pltpu.CompilerParams(collective_id=0, has_side_effects=True),
        )(
            normalized.reshape(examples, tokens, features),
            upstream.reshape(examples, tokens, features),
            owner_order,
            jnp.swapaxes(sketch_index, 1, 2),
            jnp.swapaxes(sketch_scale, 1, 2),
            query_sketch,
        )
        sketch, scores = pl.pallas_call(
            put_out,
            out_shape=(
                jax.ShapeDtypeStruct(sketch.shape, sketch.dtype),
                jax.ShapeDtypeStruct(scores.shape, scores.dtype),
            ),
            in_specs=[vmem, vmem],
            out_specs=(hbm, hbm),
            scratch_shapes=[dma((2,))],
            compiler_params=pltpu.CompilerParams(vmem_limit_bytes=1 << 20),
        )(sketch, scores)
        return sketch, scores.T

    placed = (
        P("ex", "lay", None, "col"),
        P("ex", "lay", None, "col"),
        P("ex", None),
        P(None, "col", None),
        P(None, "col", None),
        P("ex", "col"),
    )
    return jax.shard_map(
        local,
        mesh=mesh,
        in_specs=placed,
        out_specs=(P(("ex", "lay"), "col"), P(("ex", "lay"), "col")),
        check_vma=False,
    )
```

```python
import functools
import math

import jax
import jax.numpy as jnp
from jax import lax
from jax.experimental import pallas as pl
from jax.experimental.pallas import tpu as pltpu
from jax.sharding import PartitionSpec as P

MESH = pl.DeviceIdType.MESH
LANES = 128
WAVES = 4
TILE = 16
CUTS = 2
PUT = 8


def cuts(total):
    waves = min(WAVES, total)
    sizes = [total // waves + (i < total % waves) for i in range(waves)]
    return [(sum(sizes[:i]), sizes[i]) for i in range(waves)]


def batches(waves):
    heads = [(*waves[0], [0])]
    tail = waves[1:]
    if tail:
        heads.append((tail[0][0], sum(count for _, count in tail), list(range(1, len(waves)))))
    return heads


def signs():
    bits = lax.broadcasted_iota(jnp.int32, (LANES, LANES), 0) & lax.broadcasted_iota(
        jnp.int32, (LANES, LANES), 1
    )
    bits = bits ^ (bits >> 4)
    bits = bits ^ (bits >> 2)
    bits = bits ^ (bits >> 1)
    return (1 - 2 * (bits & 1)).astype(jnp.float32).astype(jnp.bfloat16)


def kernel(
    sizes,
    x_hbm,
    u_hbm,
    order_hbm,
    index_hbm,
    scale_hbm,
    query_hbm,
    sketch_ref,
    scores_ref,
    order_ref,
    index_ref,
    scale_ref,
    query_ref,
    xu_ref,
    owned_ref,
    arrived_ref,
    sibling_ref,
    own_tab_ref,
    tabs_ref,
    own_query_f32_ref,
    own_query_ref,
    queries_ref,
    had_ref,
    splat_ref,
    turned_tab_ref,
    weights_ref,
    wide_ref,
    mix_ref,
    total_ref,
    score_ref,
    load_sem,
    small_sem,
    send_sem,
    wave_sem,
    sibling_sem,
    tab_sem,
    query_sem,
    ready_sem,
):
    n_ex, n_col, n_lay, per_col, k_sel = sizes
    ex, col, lay = lax.axis_index("ex"), lax.axis_index("col"), lax.axis_index("lay")
    examples, tokens, features = x_hbm.shape
    pack = TILE // tokens
    rows = examples // n_lay
    in_blocks = features // LANES
    layers = index_ref.shape[0]
    stride = LANES // layers
    out_blocks = query_ref.shape[1] // LANES
    half = n_col // 2
    others = n_lay * half - 1
    core, chip = lax.rem(col, 2), lay * half + col // 2
    sibling = col + 1 - 2 * core
    scale = 1.0 / math.sqrt(float(LANES))
    waves = cuts(in_blocks)

    parts = batches(waves)
    load_parts = [pl.ds(first * LANES, count * LANES) for first, count, _ in parts]
    smalls = [
        pltpu.make_async_copy(source, held, small_sem.at[i])
        for i, (source, held) in enumerate(
            [
                (order_hbm, order_ref),
                (index_hbm, index_ref),
                (scale_hbm, scale_ref),
                (query_hbm, query_ref),
            ]
        )
    ]
    smalls[0].start()
    for k, part in enumerate(load_parts):
        for i, source in enumerate((x_hbm, u_hbm)):
            split = source.reshape(examples // pack, pack, tokens, features)
            for r in range(pack):
                pltpu.make_async_copy(
                    split.at[:, r, :, part],
                    xu_ref.at[i, :, pl.ds(r * tokens, tokens), part],
                    load_sem.at[k],
                ).start()
        if k == 0:
            for copy in smalls[1:]:
                copy.start()

    barrier = pltpu.get_barrier_semaphore()
    asker = ex // per_col
    asked_first = col * per_col

    def greet(sem, at_ex, at_col, at_lay):
        pl.semaphore_signal(
            sem,
            inc=1,
            device_id={"ex": at_ex, "col": at_col, "lay": at_lay},
            device_id_type=MESH,
        )

    def greet_chip(sem):
        def body(target, carry):
            for odd in range(2):
                greet(sem, ex, 2 * lax.rem(target, half) + odd, target // half)
            return carry

        return body

    greet(barrier, ex, sibling, lay)
    lax.fori_loop(chip + 1, others + 1, greet_chip(barrier), 0)

    def greet_askers(at_ex, carry):
        greet(barrier, at_ex, asker, lay)
        return carry

    def greet_sources(sem):
        def body(at_ex, carry):
            for at_col in range(n_col):
                greet(sem, at_ex, at_col, lay)
            return carry

        return body

    lax.fori_loop(ex + 1, n_ex, greet_askers, 0)
    lax.fori_loop(
        jnp.maximum(ex + 1, asked_first), asked_first + per_col, greet_sources(barrier), 0
    )
    below = jnp.clip(ex - asked_first, 0, per_col)
    greetings = 1 + 2 * chip + ex + n_col * below

    pl.semaphore_wait(barrier, greetings)
    lax.fori_loop(0, chip, greet_chip(ready_sem.at[1]), 0)
    lax.fori_loop(
        asked_first, jnp.minimum(asked_first + per_col, ex), greet_sources(ready_sem.at[0]), 0
    )

    had_ref[...] = signs()
    own_tab_ref[...] = jnp.full(own_tab_ref.shape, -1.0, jnp.float32)

    def turn(stacked):
        return jnp.dot(stacked, had_ref[...], preferred_element_type=jnp.float32)

    def wave_part(k):
        first, count = waves[k]
        return pl.ds(2 * others * first, 2 * others * count)

    def piece_copy(k, number):
        first, count = waves[k]
        target = number + (chip <= number).astype(jnp.int32)
        slot = chip - (chip > target).astype(jnp.int32)
        to_lay = target // half
        return pltpu.make_async_remote_copy(
            src_ref=owned_ref.at[to_lay, pl.ds(first, count)],
            dst_ref=arrived_ref.at[
                pl.ds(2 * others * first + (2 * slot + core) * count, count)
            ],
            send_sem=send_sem.at[0],
            recv_sem=wave_sem.at[k],
            device_id={"ex": ex, "col": 2 * lax.rem(target, half) + 1, "lay": to_lay},
            device_id_type=MESH,
        )

    def to_sibling(source, target, send, recv):
        return pltpu.make_async_remote_copy(
            src_ref=source,
            dst_ref=target,
            send_sem=send,
            recv_sem=recv,
            device_id={"ex": ex, "col": sibling, "lay": lay},
            device_id_type=MESH,
        )

    def own_copy(first, count):
        part = pl.ds(first, count)
        return to_sibling(
            owned_ref.at[lay, part], sibling_ref.at[part], send_sem.at[1], sibling_sem.at[0]
        )

    def relay_copy(k):
        part = arrived_ref.at[wave_part(k)]
        return to_sibling(part, part, send_sem.at[2], wave_sem.at[k])

    def tab_copy(dc):
        return pltpu.make_async_remote_copy(
            src_ref=tabs_ref.at[0],
            dst_ref=tabs_ref.at[dc],
            send_sem=tab_sem.at[0],
            recv_sem=tab_sem.at[1],
            device_id={"ex": ex, "col": lax.rem(col + dc, n_col), "lay": lay},
            device_id_type=MESH,
        )

    def all_tabs():
        part = tabs_ref.at[pl.ds(1, n_col - 1)]
        return to_sibling(part, part, tab_sem.at[0], tab_sem.at[1])

    smalls[0].wait()
    chosen = (
        lax.broadcasted_iota(jnp.int32, (examples * tokens, examples), 0) // tokens
        == order_ref[...]
    ).astype(jnp.float32)
    chosen = chosen.T.astype(jnp.bfloat16)

    def make(k):
        first, count, _ = parts[k]
        part = load_parts[k]
        pltpu.make_async_copy(
            xu_ref.at[:, :, :, part], xu_ref.at[:, :, :, part], load_sem.at[k]
        ).wait()
        x, u = (
            xu_ref[i, :, :, first * LANES : (first + count) * LANES]
            .reshape(examples * tokens, count * LANES)
            .astype(jnp.float32)
            for i in range(2)
        )
        product = x * u
        high = product.astype(jnp.bfloat16)
        low = (product - high.astype(jnp.float32)).astype(jnp.bfloat16)
        ordered = (
            jnp.dot(chosen, high, preferred_element_type=jnp.float32)
            + jnp.dot(chosen, low, preferred_element_type=jnp.float32)
        ).astype(jnp.bfloat16)
        stacked = jnp.concatenate(
            [ordered[:, b * LANES : (b + 1) * LANES] for b in range(count)], axis=0
        )
        stacked = turn(stacked).astype(jnp.bfloat16)
        for owner in range(n_lay):
            for b in range(count):
                at = b * examples + owner * rows
                owned_ref[owner, first + b] = stacked[at : at + rows]

    place = lax.rem(ex, per_col) * n_col + col
    mine = asker == col

    def query_copy(target):
        return pltpu.make_async_remote_copy(
            src_ref=own_query_ref,
            dst_ref=queries_ref.at[place],
            send_sem=query_sem.at[0],
            recv_sem=query_sem.at[1],
            device_id={"ex": target, "col": asker, "lay": lay},
            device_id_type=MESH,
        )

    def send_query(target, carry):
        query_copy(target).start()
        return carry

    def send_pieces(ks):
        def body(number, carry):
            for k in ks:
                piece_copy(k, number).start()
            return carry

        return body

    def send_first(k):
        @pl.when(chip > 0)
        def _():
            for wave in parts[k][2]:
                piece_copy(wave, 0).start()

        own_copy(*parts[k][:2]).start()

    def tabs_to(wanted):
        for dc in range(1, n_col):
            target = lax.rem(col + dc, n_col)
            pl.when(wanted(target // 2, col // 2))(lambda: tab_copy(dc).start())

    make(0)
    send_first(0)
    for copy in smalls[1:]:
        copy.wait()
    for layer in range(layers):
        at = slice(stride * layer, stride * layer + in_blocks)
        own_tab_ref[0:k_sel, at] = index_ref[layer].astype(jnp.float32)
        own_tab_ref[k_sel : 2 * k_sel, at] = scale_ref[layer].astype(jnp.float32)
    tabs_ref[0] = own_tab_ref[...].astype(jnp.bfloat16)
    for o in range(out_blocks):
        own_query_f32_ref[o : o + 1, :] = query_ref[:, o * LANES : (o + 1) * LANES].astype(
            jnp.float32
        )
    own_query_ref[...] = own_query_f32_ref[...].astype(jnp.bfloat16)
    tabs_to(lambda target, here: target <= here)
    def share_query():
        query_copy(ex).start()

    here = asker // 2 <= col // 2

    @pl.when(mine)
    def _():
        pltpu.make_async_copy(own_query_ref, queries_ref.at[place], query_sem.at[1]).start()

    pl.when(jnp.logical_and(here, jnp.logical_not(mine)))(share_query)

    for k in range(1, len(parts)):
        make(k)
        send_first(k)


    lax.fori_loop(1, chip, send_pieces(range(len(waves))), 0)

    @pl.when(chip < others)
    def _():
        pl.semaphore_wait(ready_sem.at[1], 2 * (others - chip))
        tabs_to(lambda target, here: target > here)
        lax.fori_loop(chip, others, send_pieces(range(len(waves))), 0)
        pl.when(jnp.logical_not(here))(share_query)

    lax.fori_loop(0, ex, send_query, 0)

    def queries_up():
        @pl.when(ex < n_ex - 1)
        def _():
            pl.semaphore_wait(ready_sem.at[0], n_ex - 1 - ex)
            lax.fori_loop(ex + 1, n_ex, send_query, 0)

    def slot_of(source):
        return lax.rem(col - source + n_col, n_col)

    def table(slot, first, count):
        tab = tabs_ref[slot].astype(jnp.float32)
        targets = (first + lax.broadcasted_iota(jnp.int32, (count, LANES), 0)).astype(jnp.float32)
        value = jnp.zeros((count, LANES), jnp.float32)
        for k in range(k_sel):
            value = value + jnp.where(
                targets == tab[k : k + 1, :], tab[k_sel + k : k_sel + k + 1, :], 0.0
            )
        return value

    def spread(slot):
        own = table(slot, col * out_blocks, out_blocks)
        for at_lay in range(layers):
            for b in range(in_blocks):
                at = stride * at_lay + b
                splat_ref[at_lay, slot, b] = jnp.broadcast_to(
                    own[:, at : at + 1], (out_blocks, LANES)
                )

    edge = min(rows, TILE)
    folds = rows // edge
    across = LANES // edge
    metas, bases = [], {}

    def prepare(name, blocks):
        base = sum(-(-len(held) // across) for held, _, _ in bases.values())
        bases[name] = (blocks, base, len(metas))
        metas.extend(blocks)
        lane = lax.broadcasted_iota(jnp.int32, (out_blocks, LANES), 1) // edge
        same = lax.rem(lax.broadcasted_iota(jnp.int32, (edge, LANES), 1), edge) == (
            lax.broadcasted_iota(jnp.int32, (edge, LANES), 0)
        )
        for t in range(0, len(blocks), across):
            wide = jnp.zeros((out_blocks, LANES), jnp.float32)
            for i, (at_lay, slot, b) in enumerate(blocks[t : t + across]):
                wide = jnp.where(lane == i, splat_ref[at_lay, slot, b], wide)
            tile = base + t // across
            wide_ref[tile] = wide
            for o in range(out_blocks):
                mix_ref[tile, o * edge : (o + 1) * edge, :] = jnp.where(
                    same, jnp.broadcast_to(wide_ref[tile, o : o + 1, :], (edge, LANES)), 0.0
                ).astype(jnp.bfloat16)

    def combine(name, source, first=False, last=False):
        blocks, base, _ = bases[name]
        folded = jnp.concatenate(
            [
                source[:, h * edge : (h + 1) * edge, :].reshape(len(blocks) * edge, LANES)
                for h in range(folds)
            ],
            axis=1,
        )
        cut = out_blocks // CUTS
        for low in range(0, out_blocks, cut):
            part = slice(low * edge, (low + cut) * edge)
            value = None
            for t in range(0, len(blocks), across):
                width = min(across, len(blocks) - t) * edge
                term = jnp.dot(
                    mix_ref[base + t // across, part, :width],
                    folded[t * edge : t * edge + width],
                    preferred_element_type=jnp.float32,
                )
                value = term if value is None else value + term
            if not first:
                value = value + total_ref[part]
            if not last:
                total_ref[part] = value
                continue
            value = value * scale
            for o in range(cut):
                at = slice((low + o) * LANES, (low + o + 1) * LANES)
                for h in range(folds):
                    sketch_ref[h * edge : (h + 1) * edge, at] = value[
                        o * edge : (o + 1) * edge, h * LANES : (h + 1) * LANES
                    ].astype(jnp.bfloat16)

    def await_wave(k):
        part = arrived_ref.at[wave_part(k)]
        to_sibling(part, part, send_sem.at[2], wave_sem.at[k]).wait_recv()

    def wave_blocks(k):
        first, count = waves[k]
        blocks = []
        for number in range(others):
            source = number + (chip <= number).astype(jnp.int32)
            for odd in range(2):
                slot = slot_of(2 * lax.rem(source, half) + odd)
                blocks += [(source // half, slot, first + b) for b in range(count)]
        return blocks

    def add_scores(name, source):
        blocks = bases[name][0]
        for q in range(per_col):
            value = score_ref[q]
            for i, (at_lay, slot, b) in enumerate(blocks):
                value = value + source[i].astype(jnp.float32) * weights_ref[
                    slot, at_lay, b : b + 1, q * LANES : (q + 1) * LANES
                ]
            score_ref[q] = value

    def wave_values(k):
        first, count = waves[k]
        low = 2 * others * first
        return arrived_ref[low : low + 2 * others * count]

    spread(0)
    prepare("own", [(lay, 0, b) for b in range(in_blocks)])
    combine("own", owned_ref[lay], first=True)
    near = slot_of(sibling)

    odd_core = core == 1

    def take(k):
        await_wave(k)
        relay_copy(k).start()

    pl.when(chip > 0)(queries_up)
    pl.when(odd_core)(lambda: take(0))

    all_tabs().wait_recv()
    for slot in range(1, n_col):
        spread(slot)
    prepare("sibling", [(lay, near, b) for b in range(in_blocks)])
    for k in range(len(waves)):
        prepare(k, wave_blocks(k))
    to_sibling(sibling_ref, sibling_ref, send_sem.at[1], sibling_sem.at[0]).wait_recv()
    combine("sibling", sibling_ref[...])
    for slot in range(n_col):
        whole = table(slot, 0, n_col * out_blocks).T
        turned_tab_ref[slot] = whole.astype(jnp.bfloat16)

    def put_scores():
        for q in range(per_col):
            scores_ref[q : q + 1, :] = jnp.sum(score_ref[q].T, axis=0, keepdims=True) * scale

    def start_scores():
        pltpu.make_async_copy(queries_ref, queries_ref, query_sem.at[1]).wait()
        asked = jnp.concatenate(
            [
                queries_ref[j * n_col : (j + 1) * n_col]
                .astype(jnp.float32)
                .reshape(n_col * out_blocks, LANES)
                for j in range(per_col)
            ],
            axis=1,
        ).astype(jnp.bfloat16)
        weights_ref[...] = jnp.dot(
            turned_tab_ref[...].reshape(n_col * LANES, n_col * out_blocks),
            asked,
            preferred_element_type=jnp.float32,
        ).reshape(weights_ref.shape)
        score_ref[...] = jnp.zeros_like(score_ref)
        add_scores("own", owned_ref[lay])
        add_scores("sibling", sibling_ref[...])

    timely = asked_first >= ex

    @pl.when(jnp.logical_not(timely))
    def _():
        weights_ref[...] = jnp.zeros_like(weights_ref)
        score_ref[...] = jnp.zeros_like(score_ref)

    pl.when(jnp.logical_and(timely, jnp.logical_not(odd_core)))(start_scores)
    pl.when(chip == 0)(queries_up)
    last = len(waves) - 1
    for k in range(len(waves)):
        if k == 0:

            @pl.when(odd_core)
            def _():
                for later in range(1, len(waves)):
                    take(later)
                pl.when(timely)(start_scores)

        pl.when(jnp.logical_not(odd_core))(lambda: await_wave(k))
        if k == last:
            add_scores(k, wave_values(k))
            put_scores()
        combine(k, wave_values(k), last=k == last)
        if k < last:
            add_scores(k, wave_values(k))

    @pl.when(jnp.logical_not(timely))
    def _():
        start_scores()
        for k in range(len(waves)):
            add_scores(k, wave_values(k))
        put_scores()

    part = arrived_ref.at[pl.ds(0, others * in_blocks)]
    to_sibling(part, part, send_sem.at[0], wave_sem.at[0]).wait_send()
    to_sibling(sibling_ref, sibling_ref, send_sem.at[1], sibling_sem.at[0]).wait_send()
    all_tabs().wait_send()

    @pl.when(odd_core)
    def _():
        to_sibling(arrived_ref, arrived_ref, send_sem.at[2], wave_sem.at[0]).wait_send()

    def sent_queries(count):
        part = queries_ref.at[pl.ds(0, count)]
        to_sibling(part, part, query_sem.at[0], query_sem.at[1]).wait_send()

    pl.when(jnp.logical_not(mine))(lambda: sent_queries(n_ex))
    if n_ex > 1:
        pl.when(mine)(lambda: sent_queries(n_ex - 1))


def put_out(sketch_ref, scores_ref, sketch_hbm, scores_hbm, sem):
    for first in range(0, sketch_ref.shape[0], PUT):
        part = pl.ds(first, PUT)
        pltpu.make_async_copy(sketch_ref.at[part], sketch_hbm.at[part], sem.at[0]).start()
    scores = pltpu.make_async_copy(scores_ref, scores_hbm, sem.at[1])
    scores.start()
    pltpu.make_async_copy(sketch_ref, sketch_hbm, sem.at[0]).wait()
    scores.wait()


def solution(mesh):
    n_ex, n_col, n_lay = (mesh.shape[name] for name in ("ex", "col", "lay"))

    def local(normalized, upstream, owner_order, sketch_index, sketch_scale, query_sketch):
        examples, own_layers, tokens, features = normalized.shape
        layers, in_blocks, k_sel = sketch_index.shape
        width = query_sketch.shape[1]
        out_blocks = width // LANES
        assert TILE % tokens == 0 and examples * tokens % TILE == 0
        assert own_layers == 1 and query_sketch.shape[0] == 1 and n_col % 2 == 0
        assert n_col * out_blocks <= 256 and in_blocks <= LANES // layers
        per_col = n_ex // n_col
        rows = examples // n_lay
        waves = len(cuts(in_blocks))
        others = n_lay * n_col // 2 - 1
        edge = min(rows, TILE)
        groups = [in_blocks] * 2 + [2 * others * count for _, count in cuts(in_blocks)]
        tiles = sum(-(-blocks * edge // LANES) for blocks in groups)
        vmem = pl.BlockSpec(memory_space=pltpu.VMEM)
        hbm = pl.BlockSpec(memory_space=pl.ANY)
        dma = pltpu.SemaphoreType.DMA
        sketch, scores = pl.pallas_call(
            functools.partial(kernel, (n_ex, n_col, n_lay, per_col, k_sel)),
            out_shape=(
                pltpu.VMEM((rows, width), jnp.bfloat16),
                pltpu.VMEM((per_col, rows), jnp.float32),
            ),
            in_specs=[hbm] * 6,
            out_specs=(vmem, vmem),
            scratch_shapes=[
                pltpu.VMEM(owner_order.shape, jnp.int32),
                pltpu.VMEM((layers, k_sel, in_blocks), jnp.int32),
                pltpu.VMEM((layers, k_sel, in_blocks), jnp.bfloat16),
                pltpu.VMEM(query_sketch.shape, jnp.bfloat16),
                pltpu.VMEM((2, examples * tokens // TILE, TILE, features), jnp.bfloat16),
                pltpu.VMEM((n_lay, in_blocks, rows, LANES), jnp.bfloat16),
                pltpu.VMEM((2 * others * in_blocks, rows, LANES), jnp.bfloat16),
                pltpu.VMEM((in_blocks, rows, LANES), jnp.bfloat16),
                pltpu.VMEM((2 * k_sel, LANES), jnp.float32),
                pltpu.VMEM((n_col, 2 * k_sel, LANES), jnp.bfloat16),
                pltpu.VMEM((out_blocks, LANES), jnp.float32),
                pltpu.VMEM((out_blocks, LANES), jnp.bfloat16),
                pltpu.VMEM((n_ex, out_blocks, LANES), jnp.bfloat16),
                pltpu.VMEM((LANES, LANES), jnp.bfloat16),
                pltpu.VMEM((layers, n_col, in_blocks, out_blocks, LANES), jnp.float32),
                pltpu.VMEM((n_col, LANES, n_col * out_blocks), jnp.bfloat16),
                pltpu.VMEM((n_col, layers, LANES // layers, per_col * LANES), jnp.float32),
                pltpu.VMEM((tiles, out_blocks, LANES), jnp.float32),
                pltpu.VMEM((tiles, out_blocks * edge, LANES), jnp.bfloat16),
                pltpu.VMEM((out_blocks * edge, rows // edge * LANES), jnp.float32),
                pltpu.VMEM((per_col, rows, LANES), jnp.float32),
                dma((min(waves, 2),)),
                dma((4,)),
                dma((3,)),
                dma((waves,)),
                dma((1,)),
                dma((2,)),
                dma((2,)),
                pltpu.SemaphoreType.REGULAR((2,)),
            ],
            compiler_params=pltpu.CompilerParams(collective_id=0, has_side_effects=True),
        )(
            normalized.reshape(examples, tokens, features),
            upstream.reshape(examples, tokens, features),
            owner_order,
            jnp.swapaxes(sketch_index, 1, 2),
            jnp.swapaxes(sketch_scale, 1, 2),
            query_sketch,
        )
        sketch, scores = pl.pallas_call(
            put_out,
            out_shape=(
                jax.ShapeDtypeStruct(sketch.shape, sketch.dtype),
                jax.ShapeDtypeStruct(scores.shape, scores.dtype),
            ),
            in_specs=[vmem, vmem],
            out_specs=(hbm, hbm),
            scratch_shapes=[dma((2,))],
            compiler_params=pltpu.CompilerParams(vmem_limit_bytes=1 << 20),
        )(sketch, scores)
        return sketch, scores.T

    placed = (
        P("ex", "lay", None, "col"),
        P("ex", "lay", None, "col"),
        P("ex", None),
        P(None, "col", None),
        P(None, "col", None),
        P("ex", "col"),
    )
    return jax.shard_map(
        local,
        mesh=mesh,
        in_specs=placed,
        out_specs=(P(("ex", "lay"), "col"), P(("ex", "lay"), "col")),
        check_vma=False,
    )
```

```python
import functools
import math

import jax
import jax.numpy as jnp
from jax import lax
from jax.experimental import pallas as pl
from jax.experimental.pallas import tpu as pltpu
from jax.sharding import PartitionSpec as P

MESH = pl.DeviceIdType.MESH
LANES = 128
WAVES = 4
TILE = 16
CUTS = 2
PUT = 8


def cuts(total):
    waves = min(WAVES, total)
    sizes = [total // waves + (i < total % waves) for i in range(waves)]
    return [(sum(sizes[:i]), sizes[i]) for i in range(waves)]


def batches(waves):
    heads = [(*waves[0], [0])]
    tail = waves[1:]
    if tail:
        heads.append((tail[0][0], sum(count for _, count in tail), list(range(1, len(waves)))))
    return heads


def signs():
    bits = lax.broadcasted_iota(jnp.int32, (LANES, LANES), 0) & lax.broadcasted_iota(
        jnp.int32, (LANES, LANES), 1
    )
    bits = bits ^ (bits >> 4)
    bits = bits ^ (bits >> 2)
    bits = bits ^ (bits >> 1)
    return (1 - 2 * (bits & 1)).astype(jnp.float32).astype(jnp.bfloat16)


def kernel(
    sizes,
    x_hbm,
    u_hbm,
    order_hbm,
    index_hbm,
    scale_hbm,
    query_hbm,
    sketch_ref,
    scores_ref,
    order_ref,
    index_ref,
    scale_ref,
    query_ref,
    xu_ref,
    owned_ref,
    arrived_ref,
    sibling_ref,
    own_tab_ref,
    tabs_ref,
    own_query_f32_ref,
    own_query_ref,
    queries_ref,
    had_ref,
    splat_ref,
    turned_tab_ref,
    weights_ref,
    wide_ref,
    mix_ref,
    total_ref,
    score_ref,
    load_sem,
    small_sem,
    send_sem,
    wave_sem,
    sibling_sem,
    tab_sem,
    query_sem,
    ready_sem,
):
    n_ex, n_col, n_lay, per_col, k_sel = sizes
    ex, col, lay = lax.axis_index("ex"), lax.axis_index("col"), lax.axis_index("lay")
    examples, tokens, features = x_hbm.shape
    pack = TILE // tokens
    rows = examples // n_lay
    in_blocks = features // LANES
    layers = index_ref.shape[0]
    stride = LANES // layers
    padded = weights_ref.shape[2]
    out_blocks = query_ref.shape[1] // LANES
    half = n_col // 2
    others = n_lay * half - 1
    core, chip = lax.rem(col, 2), lay * half + col // 2
    sibling = col + 1 - 2 * core
    scale = 1.0 / math.sqrt(float(LANES))
    waves = cuts(in_blocks)

    barrier = pltpu.get_barrier_semaphore()
    asker = ex // per_col
    asked_first = col * per_col

    def greet(sem, at_ex, at_col, at_lay):
        pl.semaphore_signal(
            sem,
            inc=1,
            device_id={"ex": at_ex, "col": at_col, "lay": at_lay},
            device_id_type=MESH,
        )

    def greet_chip(sem, target):
        for odd in range(2):
            greet(sem, ex, 2 * lax.rem(target, half) + odd, target // half)

    def greet_chips(sem, start, stop):
        def body(target, carry):
            greet_chip(sem, target)
            return carry

        lax.fori_loop(start, stop, body, 0)

    def greet_askers(at_ex, carry):
        greet(barrier, at_ex, asker, lay)
        return carry

    def greet_sources(sem):
        def body(at_ex, carry):
            for at_col in range(n_col):
                greet(sem, at_ex, at_col, lay)
            return carry

        return body

    below = jnp.clip(ex - asked_first, 0, per_col)
    greeted = jnp.where(chip == others, others, jnp.minimum(chip, 1))
    greetings = 1 + 2 * greeted + ex + n_col * below

    def known(target):
        return jnp.logical_or(
            target == chip, jnp.logical_or(chip == others, jnp.logical_and(target == 0, chip > 0))
        )

    parts = batches(waves)
    load_parts = [pl.ds(first * LANES, count * LANES) for first, count, _ in parts]
    smalls = [
        pltpu.make_async_copy(source, held, small_sem.at[i])
        for i, (source, held) in enumerate(
            [
                (order_hbm, order_ref),
                (index_hbm, index_ref),
                (scale_hbm, scale_ref),
                (query_hbm, query_ref),
            ]
        )
    ]
    smalls[0].start()
    for k, part in enumerate(load_parts):
        for i, source in enumerate((x_hbm, u_hbm)):
            split = source.reshape(examples // pack, pack, tokens, features)
            for r in range(pack):
                pltpu.make_async_copy(
                    split.at[:, r, :, part],
                    xu_ref.at[i, :, pl.ds(r * tokens, tokens), part],
                    load_sem.at[k],
                ).start()
        if k == 0:
            for copy in smalls[1:]:
                copy.start()

    pl.when(chip == 0)(lambda: greet_chips(barrier, 1, others + 1))
    pl.when(jnp.logical_and(chip > 0, chip < others))(lambda: greet_chip(barrier, others))
    greet(barrier, ex, sibling, lay)
    lax.fori_loop(ex + 1, n_ex, greet_askers, 0)
    lax.fori_loop(
        jnp.maximum(ex + 1, asked_first), asked_first + per_col, greet_sources(barrier), 0
    )
    pl.semaphore_wait(barrier, greetings)
    pl.when(jnp.logical_and(chip > 0, chip < others))(lambda: greet_chip(ready_sem.at[1], 0))
    pl.when(chip == others)(lambda: greet_chips(ready_sem.at[1], 0, others))
    lax.fori_loop(
        asked_first, jnp.minimum(asked_first + per_col, ex), greet_sources(ready_sem.at[0]), 0
    )

    had_ref[...] = signs()
    own_tab_ref[...] = jnp.full(own_tab_ref.shape, -1.0, jnp.float32)

    def turn(stacked):
        return jnp.dot(stacked, had_ref[...], preferred_element_type=jnp.float32)

    def wave_part(k):
        first, count = waves[k]
        return pl.ds(2 * others * first, 2 * others * count)

    def piece_copy(k, number):
        first, count = waves[k]
        target = number + (chip <= number).astype(jnp.int32)
        slot = chip - (chip > target).astype(jnp.int32)
        to_lay = target // half
        return pltpu.make_async_remote_copy(
            src_ref=owned_ref.at[to_lay, pl.ds(first, count)],
            dst_ref=arrived_ref.at[
                pl.ds(2 * others * first + (2 * slot + core) * count, count)
            ],
            send_sem=send_sem.at[0],
            recv_sem=wave_sem.at[k],
            device_id={"ex": ex, "col": 2 * lax.rem(target, half) + 1, "lay": to_lay},
            device_id_type=MESH,
        )

    def to_sibling(source, target, send, recv):
        return pltpu.make_async_remote_copy(
            src_ref=source,
            dst_ref=target,
            send_sem=send,
            recv_sem=recv,
            device_id={"ex": ex, "col": sibling, "lay": lay},
            device_id_type=MESH,
        )

    def own_copy(first, count):
        part = pl.ds(first, count)
        return to_sibling(
            owned_ref.at[lay, part], sibling_ref.at[part], send_sem.at[0], sibling_sem.at[0]
        )

    def relay_copy(k):
        part = arrived_ref.at[wave_part(k)]
        return to_sibling(part, part, send_sem.at[1], wave_sem.at[k])

    def tab_copy(dc):
        return pltpu.make_async_remote_copy(
            src_ref=tabs_ref.at[0],
            dst_ref=tabs_ref.at[dc],
            send_sem=tab_sem.at[0],
            recv_sem=tab_sem.at[1],
            device_id={"ex": ex, "col": lax.rem(col + dc, n_col), "lay": lay},
            device_id_type=MESH,
        )

    def all_tabs():
        part = tabs_ref.at[pl.ds(1, n_col - 1)]
        return to_sibling(part, part, tab_sem.at[0], tab_sem.at[1])

    smalls[0].wait()
    chosen = (
        lax.broadcasted_iota(jnp.int32, (examples * tokens, examples), 0) // tokens
        == order_ref[...]
    ).astype(jnp.float32)
    chosen = chosen.T.astype(jnp.bfloat16)

    def make(k):
        first, count, _ = parts[k]
        part = load_parts[k]
        pltpu.make_async_copy(
            xu_ref.at[:, :, :, part], xu_ref.at[:, :, :, part], load_sem.at[k]
        ).wait()
        ordered = []
        for b in range(first, first + count):
            x, u = (
                xu_ref[i, :, :, b * LANES : (b + 1) * LANES]
                .reshape(examples * tokens, LANES)
                .astype(jnp.float32)
                for i in range(2)
            )
            product = x * u
            high = product.astype(jnp.bfloat16)
            low = (product - high.astype(jnp.float32)).astype(jnp.bfloat16)
            ordered.append(
                (
                    jnp.dot(chosen, high, preferred_element_type=jnp.float32)
                    + jnp.dot(chosen, low, preferred_element_type=jnp.float32)
                ).astype(jnp.bfloat16)
            )
        for b in range(count):
            stacked = turn(ordered[b]).astype(jnp.bfloat16)
            for owner in range(n_lay):
                owned_ref[owner, first + b] = stacked[owner * rows : (owner + 1) * rows]

    place = lax.rem(ex, per_col) * n_col + col
    mine = asker == col

    def query_copy(target):
        return pltpu.make_async_remote_copy(
            src_ref=own_query_ref,
            dst_ref=queries_ref.at[place],
            send_sem=query_sem.at[0],
            recv_sem=query_sem.at[1],
            device_id={"ex": target, "col": asker, "lay": lay},
            device_id_type=MESH,
        )

    def send_query(target, carry):
        query_copy(target).start()
        return carry

    def send_pieces(ks):
        def body(number, carry):
            for k in ks:
                piece_copy(k, number).start()
            return carry

        return body

    def send_first(k):
        @pl.when(chip > 0)
        def _():
            for wave in parts[k][2]:
                piece_copy(wave, 0).start()

        own_copy(*parts[k][:2]).start()

    def tabs_to(greeted):
        for dc in range(1, n_col):
            target = lay * half + lax.rem(col + dc, n_col) // 2
            pl.when(known(target) == greeted)(lambda: tab_copy(dc).start())

    make(0)
    send_first(0)
    for copy in smalls[1:]:
        copy.wait()
    for layer in range(layers):
        at = slice(stride * layer, stride * layer + in_blocks)
        own_tab_ref[0:k_sel, at] = index_ref[layer].astype(jnp.float32)
        own_tab_ref[k_sel : 2 * k_sel, at] = scale_ref[layer].astype(jnp.float32)
    tabs_ref[0] = own_tab_ref[...].astype(jnp.bfloat16)
    for o in range(out_blocks):
        own_query_f32_ref[o : o + 1, :] = query_ref[:, o * LANES : (o + 1) * LANES].astype(
            jnp.float32
        )
    own_query_ref[...] = own_query_f32_ref[...].astype(jnp.bfloat16)
    tabs_to(True)
    def share_query():
        query_copy(ex).start()

    here = known(lay * half + asker // 2)

    @pl.when(mine)
    def _():
        pltpu.make_async_copy(own_query_ref, queries_ref.at[place], query_sem.at[1]).start()

    pl.when(jnp.logical_and(here, jnp.logical_not(mine)))(share_query)

    for k in range(1, len(parts)):
        make(k)
        send_first(k)


    @pl.when(chip < others)
    def _():
        pl.semaphore_wait(ready_sem.at[1], jnp.where(chip == 0, 2 * others, 2))
        tabs_to(False)
        pl.when(jnp.logical_not(here))(share_query)

        lax.fori_loop(jnp.minimum(chip, 1), others, send_pieces(range(len(waves))), 0)

    lax.fori_loop(0, ex, send_query, 0)

    def queries_up():
        @pl.when(ex < n_ex - 1)
        def _():
            pl.semaphore_wait(ready_sem.at[0], n_ex - 1 - ex)
            lax.fori_loop(ex + 1, n_ex, send_query, 0)

    def slot_of(source):
        return lax.rem(col - source + n_col, n_col)

    def table(slot, first, count):
        tab = tabs_ref[slot].astype(jnp.float32)
        targets = (first + lax.broadcasted_iota(jnp.int32, (count, LANES), 0)).astype(jnp.float32)
        value = jnp.zeros((count, LANES), jnp.float32)
        for k in range(k_sel):
            value = value + jnp.where(
                targets == tab[k : k + 1, :], tab[k_sel + k : k_sel + k + 1, :], 0.0
            )
        return value

    def spread(slot):
        own = table(slot, col * out_blocks, out_blocks)
        for at_lay in range(layers):
            for b in range(in_blocks):
                at = stride * at_lay + b
                splat_ref[at_lay, slot, b] = jnp.broadcast_to(
                    own[:, at : at + 1], (out_blocks, LANES)
                )

    edge = min(rows, TILE)
    folds = rows // edge
    across = LANES // edge
    metas, bases = [], {}

    def prepare(name, blocks):
        base = sum(-(-len(held) // across) for held, _, _ in bases.values())
        bases[name] = (blocks, base, len(metas))
        metas.extend(blocks)
        lane = lax.broadcasted_iota(jnp.int32, (out_blocks, LANES), 1) // edge
        same = lax.rem(lax.broadcasted_iota(jnp.int32, (edge, LANES), 1), edge) == (
            lax.broadcasted_iota(jnp.int32, (edge, LANES), 0)
        )
        for t in range(0, len(blocks), across):
            wide = jnp.zeros((out_blocks, LANES), jnp.float32)
            for i, (at_lay, slot, b) in enumerate(blocks[t : t + across]):
                wide = jnp.where(lane == i, splat_ref[at_lay, slot, b], wide)
            tile = base + t // across
            wide_ref[tile] = wide
            for o in range(out_blocks):
                mix_ref[tile, o * edge : (o + 1) * edge, :] = jnp.where(
                    same, jnp.broadcast_to(wide_ref[tile, o : o + 1, :], (edge, LANES)), 0.0
                ).astype(jnp.bfloat16)

    cut = out_blocks // CUTS
    cut_rows = [slice(low * edge, (low + cut) * edge) for low in range(0, out_blocks, cut)]

    def combine(name, source, sums):
        blocks, base, _ = bases[name]
        folded = jnp.concatenate(
            [
                source[:, h * edge : (h + 1) * edge, :].reshape(len(blocks) * edge, LANES)
                for h in range(folds)
            ],
            axis=1,
        )
        result = []
        for part, value in zip(cut_rows, sums):
            for t in range(0, len(blocks), across):
                width = min(across, len(blocks) - t) * edge
                term = jnp.dot(
                    mix_ref[base + t // across, part, :width],
                    folded[t * edge : t * edge + width],
                    preferred_element_type=jnp.float32,
                )
                value = term if value is None else value + term
            result.append(value)
        return result

    def put_sketch(sums):
        for i, value in enumerate(sums):
            value = (value + total_ref[cut_rows[i]]) * scale
            at = slice(cut * i * LANES, cut * (i + 1) * LANES)
            for h in range(folds):
                for r in range(0, edge, PUT):
                    sketch_ref[h * edge + r : h * edge + r + PUT, at] = jnp.concatenate(
                        [
                            value[o * edge + r : o * edge + r + PUT, h * LANES : (h + 1) * LANES]
                            for o in range(cut)
                        ],
                        axis=1,
                    ).astype(jnp.bfloat16)

    def await_wave(k):
        part = arrived_ref.at[wave_part(k)]
        to_sibling(part, part, send_sem.at[1], wave_sem.at[k]).wait_recv()

    def wave_blocks(k):
        first, count = waves[k]
        blocks = []
        for number in range(others):
            source = number + (chip <= number).astype(jnp.int32)
            for odd in range(2):
                slot = slot_of(2 * lax.rem(source, half) + odd)
                blocks += [(source // half, slot, first + b) for b in range(count)]
        return blocks

    def add_scores(name, source):
        blocks, values = bases[name][0], []
        for q in range(per_col):
            value = score_ref[q]
            for i, (at_lay, slot, b) in enumerate(blocks):
                value = value + source[i].astype(jnp.float32) * weights_ref[
                    slot, at_lay, b : b + 1, q * LANES : (q + 1) * LANES
                ]
            score_ref[q] = value
            values.append(value)
        return values

    def wave_values(k):
        first, count = waves[k]
        low = 2 * others * first
        return arrived_ref[low : low + 2 * others * count]

    spread(0)
    prepare("own", [(lay, 0, b) for b in range(in_blocks)])
    none = [None] * CUTS
    for part, value in zip(cut_rows, combine("own", owned_ref[lay], none)):
        total_ref[part] = value
    @pl.when(chip == others)
    def _():
        lax.fori_loop(1, others, send_pieces(range(len(waves))), 0)

    near = slot_of(sibling)

    odd_core = core == 1

    def take(k):
        await_wave(k)
        relay_copy(k).start()

    pl.when(chip > 0)(queries_up)
    pl.when(odd_core)(lambda: take(0))

    all_tabs().wait_recv()
    for slot in range(1, n_col):
        spread(slot)
    prepare("sibling", [(lay, near, b) for b in range(in_blocks)])
    for k in range(len(waves)):
        prepare(k, wave_blocks(k))
    to_sibling(sibling_ref, sibling_ref, send_sem.at[0], sibling_sem.at[0]).wait_recv()
    for part, value in zip(cut_rows, combine("sibling", sibling_ref[...], none)):
        total_ref[part] = total_ref[part] + value
    for slot in range(n_col):
        whole = table(slot, 0, n_col * out_blocks).T
        for at_lay in range(layers):
            at = stride * at_lay
            turned_tab_ref[slot, at_lay] = whole[at : at + padded].astype(jnp.bfloat16)

    def put_scores(values):
        for q, value in enumerate(values):
            scores_ref[q : q + 1, :] = jnp.sum(value.T, axis=0, keepdims=True) * scale

    def start_scores():
        pltpu.make_async_copy(queries_ref, queries_ref, query_sem.at[1]).wait()
        asked = jnp.concatenate(
            [
                queries_ref[j * n_col : (j + 1) * n_col].reshape(n_col * out_blocks, LANES)
                for j in range(per_col)
            ],
            axis=1,
        )
        weights_ref[...] = jnp.dot(
            turned_tab_ref[...].reshape(n_col * layers * padded, n_col * out_blocks),
            asked,
            preferred_element_type=jnp.float32,
        ).reshape(weights_ref.shape)
        score_ref[...] = jnp.zeros_like(score_ref)
        add_scores("own", owned_ref[lay])
        add_scores("sibling", sibling_ref[...])

    timely = jnp.logical_or(
        asked_first == ex, jnp.logical_and(asked_first > ex, jnp.logical_not(odd_core))
    )

    @pl.when(jnp.logical_not(timely))
    def _():
        weights_ref[...] = jnp.zeros_like(weights_ref)
        score_ref[...] = jnp.zeros_like(score_ref)

    pl.when(jnp.logical_and(timely, jnp.logical_not(odd_core)))(start_scores)
    pl.when(chip == 0)(queries_up)
    last = len(waves) - 1
    sums = none
    for k in range(len(waves)):
        if k == 0:

            @pl.when(odd_core)
            def _():
                for later in range(1, len(waves)):
                    take(later)
                pl.when(timely)(start_scores)

        pl.when(jnp.logical_not(odd_core))(lambda: await_wave(k))
        if k == last:
            put_scores(add_scores(k, wave_values(k)))
        sums = combine(k, wave_values(k), sums)
        if k == last:
            put_sketch(sums)
        if k < last:
            add_scores(k, wave_values(k))

    @pl.when(jnp.logical_not(timely))
    def _():
        start_scores()
        for k in range(len(waves)):
            values = add_scores(k, wave_values(k))
        put_scores(values)

    part = arrived_ref.at[pl.ds(0, (others + 1) * in_blocks)]
    to_sibling(part, part, send_sem.at[0], wave_sem.at[0]).wait_send()
    all_tabs().wait_send()

    @pl.when(odd_core)
    def _():
        to_sibling(arrived_ref, arrived_ref, send_sem.at[1], wave_sem.at[0]).wait_send()

    def sent_queries(count):
        part = queries_ref.at[pl.ds(0, count)]
        to_sibling(part, part, query_sem.at[0], query_sem.at[1]).wait_send()

    pl.when(jnp.logical_not(mine))(lambda: sent_queries(n_ex))
    if n_ex > 1:
        pl.when(mine)(lambda: sent_queries(n_ex - 1))


def put_out(sketch_ref, scores_ref, sketch_hbm, scores_hbm, sem):
    for first in range(0, sketch_ref.shape[0], PUT):
        part = pl.ds(first, PUT)
        pltpu.make_async_copy(sketch_ref.at[part], sketch_hbm.at[part], sem.at[0]).start()
    scores = pltpu.make_async_copy(scores_ref, scores_hbm, sem.at[1])
    scores.start()
    pltpu.make_async_copy(sketch_ref, sketch_hbm, sem.at[0]).wait()
    scores.wait()


def solution(mesh):
    n_ex, n_col, n_lay = (mesh.shape[name] for name in ("ex", "col", "lay"))

    def local(normalized, upstream, owner_order, sketch_index, sketch_scale, query_sketch):
        examples, own_layers, tokens, features = normalized.shape
        layers, in_blocks, k_sel = sketch_index.shape
        width = query_sketch.shape[1]
        out_blocks = width // LANES
        assert TILE % tokens == 0 and examples * tokens % TILE == 0
        assert own_layers == 1 and query_sketch.shape[0] == 1 and n_col % 2 == 0
        assert n_col * out_blocks <= 256 and in_blocks <= LANES // layers
        per_col = n_ex // n_col
        rows = examples // n_lay
        waves = len(cuts(in_blocks))
        others = n_lay * n_col // 2 - 1
        edge = min(rows, TILE)
        padded = LANES // layers if in_blocks > TILE else TILE
        groups = [in_blocks] * 2 + [2 * others * count for _, count in cuts(in_blocks)]
        tiles = sum(-(-blocks * edge // LANES) for blocks in groups)
        vmem = pl.BlockSpec(memory_space=pltpu.VMEM)
        hbm = pl.BlockSpec(memory_space=pl.ANY)
        dma = pltpu.SemaphoreType.DMA
        sketch, scores = pl.pallas_call(
            functools.partial(kernel, (n_ex, n_col, n_lay, per_col, k_sel)),
            out_shape=(
                pltpu.VMEM((rows, width), jnp.bfloat16),
                pltpu.VMEM((per_col, rows), jnp.float32),
            ),
            in_specs=[hbm] * 6,
            out_specs=(vmem, vmem),
            scratch_shapes=[
                pltpu.VMEM(owner_order.shape, jnp.int32),
                pltpu.VMEM((layers, k_sel, in_blocks), jnp.int32),
                pltpu.VMEM((layers, k_sel, in_blocks), jnp.bfloat16),
                pltpu.VMEM(query_sketch.shape, jnp.bfloat16),
                pltpu.VMEM((2, examples * tokens // TILE, TILE, features), jnp.bfloat16),
                pltpu.VMEM((n_lay, in_blocks, rows, LANES), jnp.bfloat16),
                pltpu.VMEM((2 * others * in_blocks, rows, LANES), jnp.bfloat16),
                pltpu.VMEM((in_blocks, rows, LANES), jnp.bfloat16),
                pltpu.VMEM((2 * k_sel, LANES), jnp.float32),
                pltpu.VMEM((n_col, 2 * k_sel, LANES), jnp.bfloat16),
                pltpu.VMEM((out_blocks, LANES), jnp.float32),
                pltpu.VMEM((out_blocks, LANES), jnp.bfloat16),
                pltpu.VMEM((n_ex, out_blocks, LANES), jnp.bfloat16),
                pltpu.VMEM((LANES, LANES), jnp.bfloat16),
                pltpu.VMEM((layers, n_col, in_blocks, out_blocks, LANES), jnp.float32),
                pltpu.VMEM((n_col, layers, padded, n_col * out_blocks), jnp.bfloat16),
                pltpu.VMEM((n_col, layers, padded, per_col * LANES), jnp.float32),
                pltpu.VMEM((tiles, out_blocks, LANES), jnp.float32),
                pltpu.VMEM((tiles, out_blocks * edge, LANES), jnp.bfloat16),
                pltpu.VMEM((out_blocks * edge, rows // edge * LANES), jnp.float32),
                pltpu.VMEM((per_col, rows, LANES), jnp.float32),
                dma((min(waves, 2),)),
                dma((4,)),
                dma((2,)),
                dma((waves,)),
                dma((1,)),
                dma((2,)),
                dma((2,)),
                pltpu.SemaphoreType.REGULAR((2,)),
            ],
            compiler_params=pltpu.CompilerParams(collective_id=0, has_side_effects=True),
        )(
            normalized.reshape(examples, tokens, features),
            upstream.reshape(examples, tokens, features),
            owner_order,
            jnp.swapaxes(sketch_index, 1, 2),
            jnp.swapaxes(sketch_scale, 1, 2),
            query_sketch,
        )
        sketch, scores = pl.pallas_call(
            put_out,
            out_shape=(
                jax.ShapeDtypeStruct(sketch.shape, sketch.dtype),
                jax.ShapeDtypeStruct(scores.shape, scores.dtype),
            ),
            in_specs=[vmem, vmem],
            out_specs=(hbm, hbm),
            scratch_shapes=[dma((2,))],
            compiler_params=pltpu.CompilerParams(vmem_limit_bytes=1 << 20),
        )(sketch, scores)
        return sketch, scores.T

    placed = (
        P("ex", "lay", None, "col"),
        P("ex", "lay", None, "col"),
        P("ex", None),
        P(None, "col", None),
        P(None, "col", None),
        P("ex", "col"),
    )
    return jax.shard_map(
        local,
        mesh=mesh,
        in_specs=placed,
        out_specs=(P(("ex", "lay"), "col"), P(("ex", "lay"), "col")),
        check_vma=False,
    )
```

```python
import functools
import math

import jax
import jax.numpy as jnp
from jax import lax
from jax.experimental import pallas as pl
from jax.experimental.pallas import tpu as pltpu
from jax.sharding import PartitionSpec as P

MESH = pl.DeviceIdType.MESH
LANES = 128
WAVES = 4
TILE = 16
CUTS = 2
PUT = 8


def cuts(total):
    waves = min(WAVES, total)
    sizes = [total // waves + (i < total % waves) for i in range(waves)]
    return [(sum(sizes[:i]), sizes[i]) for i in range(waves)]


def batches(waves):
    heads = [(*waves[0], [0])]
    tail = waves[1:]
    if tail:
        heads.append((tail[0][0], sum(count for _, count in tail), list(range(1, len(waves)))))
    return heads


def signs():
    bits = lax.broadcasted_iota(jnp.int32, (LANES, LANES), 0) & lax.broadcasted_iota(
        jnp.int32, (LANES, LANES), 1
    )
    bits = bits ^ (bits >> 4)
    bits = bits ^ (bits >> 2)
    bits = bits ^ (bits >> 1)
    return (1 - 2 * (bits & 1)).astype(jnp.float32).astype(jnp.bfloat16)


def kernel(
    sizes,
    x_hbm,
    u_hbm,
    order_hbm,
    index_hbm,
    scale_hbm,
    query_hbm,
    sketch_ref,
    scores_ref,
    order_ref,
    index_ref,
    scale_ref,
    query_ref,
    xu_ref,
    owned_ref,
    arrived_ref,
    sibling_ref,
    own_tab_ref,
    tabs_ref,
    own_query_f32_ref,
    own_query_ref,
    queries_ref,
    had_ref,
    splat_ref,
    turned_tab_ref,
    weights_ref,
    wide_ref,
    mix_ref,
    total_ref,
    score_ref,
    load_sem,
    small_sem,
    send_sem,
    wave_sem,
    sibling_sem,
    tab_sem,
    query_sem,
    ready_sem,
):
    n_ex, n_col, n_lay, per_col, k_sel = sizes
    ex, col, lay = lax.axis_index("ex"), lax.axis_index("col"), lax.axis_index("lay")
    examples, tokens, features = x_hbm.shape
    pack = TILE // tokens
    rows = examples // n_lay
    in_blocks = features // LANES
    layers = index_ref.shape[0]
    stride = LANES // layers
    padded = weights_ref.shape[2]
    out_blocks = query_ref.shape[1] // LANES
    half = n_col // 2
    others = n_lay * half - 1
    core, chip = lax.rem(col, 2), lay * half + col // 2
    sibling = col + 1 - 2 * core
    scale = 1.0 / math.sqrt(float(LANES))
    waves = cuts(in_blocks)

    barrier = pltpu.get_barrier_semaphore()
    asker = ex // per_col
    asked_first = col * per_col

    def greet(sem, at_ex, at_col, at_lay):
        pl.semaphore_signal(
            sem,
            inc=1,
            device_id={"ex": at_ex, "col": at_col, "lay": at_lay},
            device_id_type=MESH,
        )

    def greet_chip(sem, target):
        for odd in range(2):
            greet(sem, ex, 2 * lax.rem(target, half) + odd, target // half)

    def greet_chips(sem, start, stop):
        def body(target, carry):
            greet_chip(sem, target)
            return carry

        lax.fori_loop(start, stop, body, 0)

    def greet_askers(at_ex, carry):
        greet(barrier, at_ex, asker, lay)
        return carry

    def greet_sources(sem):
        def body(at_ex, carry):
            for at_col in range(n_col):
                greet(sem, at_ex, at_col, lay)
            return carry

        return body

    below = jnp.clip(ex - asked_first, 0, per_col)
    greeted = jnp.where(chip == others, others, jnp.minimum(chip, 1))
    greetings = 1 + 2 * greeted + ex + n_col * below

    def known(target):
        return jnp.logical_or(
            target == chip, jnp.logical_or(chip == others, jnp.logical_and(target == 0, chip > 0))
        )

    parts = batches(waves)
    load_parts = [pl.ds(first * LANES, count * LANES) for first, count, _ in parts]
    smalls = [
        pltpu.make_async_copy(source, held, small_sem.at[i])
        for i, (source, held) in enumerate(
            [
                (order_hbm, order_ref),
                (index_hbm, index_ref),
                (scale_hbm, scale_ref),
                (query_hbm, query_ref),
            ]
        )
    ]
    for copy in smalls:
        copy.start()
    for k, part in enumerate(load_parts):
        for i, source in enumerate((x_hbm, u_hbm)):
            tiles = examples // pack
            split = source.reshape(tiles, pack, tokens, features)
            step = tiles // 4 if k and tiles % 4 == 0 else tiles
            for low in range(0, tiles, step):
                for r in range(pack):
                    pltpu.make_async_copy(
                        split.at[pl.ds(low, step), r, :, part],
                        xu_ref.at[i, pl.ds(low, step), pl.ds(r * tokens, tokens), part],
                        load_sem.at[k],
                    ).start()

    pl.when(chip == 0)(lambda: greet_chips(barrier, 1, others + 1))
    pl.when(jnp.logical_and(chip > 0, chip < others))(lambda: greet_chip(barrier, others))
    greet(barrier, ex, sibling, lay)
    lax.fori_loop(ex + 1, n_ex, greet_askers, 0)
    lax.fori_loop(
        jnp.maximum(ex + 1, asked_first), asked_first + per_col, greet_sources(barrier), 0
    )
    pl.semaphore_wait(barrier, greetings)
    pl.when(jnp.logical_and(chip > 0, chip < others))(lambda: greet_chip(ready_sem.at[1], 0))
    pl.when(chip == others)(lambda: greet_chips(ready_sem.at[1], 0, others))
    lax.fori_loop(
        asked_first, jnp.minimum(asked_first + per_col, ex), greet_sources(ready_sem.at[0]), 0
    )

    had_ref[...] = signs()
    own_tab_ref[...] = jnp.full(own_tab_ref.shape, -1.0, jnp.float32)

    def turn(stacked):
        return jnp.dot(stacked, had_ref[...], preferred_element_type=jnp.float32)

    def wave_part(k):
        first, count = waves[k]
        return pl.ds(2 * others * first, 2 * others * count)

    def piece_copy(k, number):
        first, count = waves[k]
        target = number + (chip <= number).astype(jnp.int32)
        slot = chip - (chip > target).astype(jnp.int32)
        to_lay = target // half
        return pltpu.make_async_remote_copy(
            src_ref=owned_ref.at[to_lay, pl.ds(first, count)],
            dst_ref=arrived_ref.at[
                pl.ds(2 * others * first + (2 * slot + core) * count, count)
            ],
            send_sem=send_sem.at[0],
            recv_sem=wave_sem.at[k],
            device_id={"ex": ex, "col": 2 * lax.rem(target, half) + 1, "lay": to_lay},
            device_id_type=MESH,
        )

    def to_sibling(source, target, send, recv):
        return pltpu.make_async_remote_copy(
            src_ref=source,
            dst_ref=target,
            send_sem=send,
            recv_sem=recv,
            device_id={"ex": ex, "col": sibling, "lay": lay},
            device_id_type=MESH,
        )

    def own_copy(first, count):
        part = pl.ds(first, count)
        return to_sibling(
            owned_ref.at[lay, part], sibling_ref.at[part], send_sem.at[0], sibling_sem.at[0]
        )

    def relay_copy(k):
        part = arrived_ref.at[wave_part(k)]
        return to_sibling(part, part, send_sem.at[1], wave_sem.at[k])

    def tab_copy(dc):
        return pltpu.make_async_remote_copy(
            src_ref=tabs_ref.at[0],
            dst_ref=tabs_ref.at[dc],
            send_sem=tab_sem.at[0],
            recv_sem=tab_sem.at[1],
            device_id={"ex": ex, "col": lax.rem(col + dc, n_col), "lay": lay},
            device_id_type=MESH,
        )

    def all_tabs():
        part = tabs_ref.at[pl.ds(1, n_col - 1)]
        return to_sibling(part, part, tab_sem.at[0], tab_sem.at[1])

    smalls[0].wait()
    chosen = (
        lax.broadcasted_iota(jnp.int32, (examples * tokens, examples), 0) // tokens
        == order_ref[...]
    ).astype(jnp.float32)
    chosen = chosen.T.astype(jnp.bfloat16)

    def make(k):
        first, count, _ = parts[k]
        part = load_parts[k]
        pltpu.make_async_copy(
            xu_ref.at[:, :, :, part], xu_ref.at[:, :, :, part], load_sem.at[k]
        ).wait()
        ordered = []
        for b in range(first, first + count):
            x, u = (
                xu_ref[i, :, :, b * LANES : (b + 1) * LANES]
                .reshape(examples * tokens, LANES)
                .astype(jnp.float32)
                for i in range(2)
            )
            product = x * u
            high = product.astype(jnp.bfloat16)
            low = (product - high.astype(jnp.float32)).astype(jnp.bfloat16)
            ordered.append(
                (
                    jnp.dot(chosen, high, preferred_element_type=jnp.float32)
                    + jnp.dot(chosen, low, preferred_element_type=jnp.float32)
                ).astype(jnp.bfloat16)
            )
        for b in range(count):
            stacked = turn(ordered[b]).astype(jnp.bfloat16)
            for owner in range(n_lay):
                owned_ref[owner, first + b] = stacked[owner * rows : (owner + 1) * rows]

    place = lax.rem(ex, per_col) * n_col + col
    mine = asker == col

    def query_copy(target):
        return pltpu.make_async_remote_copy(
            src_ref=own_query_ref,
            dst_ref=queries_ref.at[place],
            send_sem=query_sem.at[0],
            recv_sem=query_sem.at[1],
            device_id={"ex": target, "col": asker, "lay": lay},
            device_id_type=MESH,
        )

    def send_query(target, carry):
        query_copy(target).start()
        return carry

    def send_pieces(ks):
        def body(number, carry):
            for k in ks:
                piece_copy(k, number).start()
            return carry

        return body

    def send_first(k):
        @pl.when(chip > 0)
        def _():
            for wave in parts[k][2]:
                piece_copy(wave, 0).start()

        own_copy(*parts[k][:2]).start()

    def tabs_to(greeted):
        for dc in range(1, n_col):
            target = lay * half + lax.rem(col + dc, n_col) // 2
            pl.when(known(target) == greeted)(lambda: tab_copy(dc).start())

    for copy in smalls[1:]:
        copy.wait()
    for layer in range(layers):
        at = slice(stride * layer, stride * layer + in_blocks)
        own_tab_ref[0:k_sel, at] = index_ref[layer].astype(jnp.float32)
        own_tab_ref[k_sel : 2 * k_sel, at] = scale_ref[layer].astype(jnp.float32)
    tabs_ref[0] = own_tab_ref[...].astype(jnp.bfloat16)
    for o in range(out_blocks):
        own_query_f32_ref[o : o + 1, :] = query_ref[:, o * LANES : (o + 1) * LANES].astype(
            jnp.float32
        )
    own_query_ref[...] = own_query_f32_ref[...].astype(jnp.bfloat16)
    tabs_to(True)
    def share_query():
        query_copy(ex).start()

    here = known(lay * half + asker // 2)

    @pl.when(mine)
    def _():
        pltpu.make_async_copy(own_query_ref, queries_ref.at[place], query_sem.at[1]).start()

    pl.when(jnp.logical_and(here, jnp.logical_not(mine)))(share_query)

    make(0)
    send_first(0)
    for k in range(1, len(parts)):
        make(k)
        send_first(k)


    @pl.when(chip < others)
    def _():
        pl.semaphore_wait(ready_sem.at[1], jnp.where(chip == 0, 2 * others, 2))
        tabs_to(False)
        pl.when(jnp.logical_not(here))(share_query)

        lax.fori_loop(jnp.minimum(chip, 1), others, send_pieces(range(len(waves))), 0)

    lax.fori_loop(0, ex, send_query, 0)

    def queries_up():
        @pl.when(ex < n_ex - 1)
        def _():
            pl.semaphore_wait(ready_sem.at[0], n_ex - 1 - ex)
            lax.fori_loop(ex + 1, n_ex, send_query, 0)

    def slot_of(source):
        return lax.rem(col - source + n_col, n_col)

    def table(slot, first, count):
        tab = tabs_ref[slot].astype(jnp.float32)
        targets = (first + lax.broadcasted_iota(jnp.int32, (count, LANES), 0)).astype(jnp.float32)
        value = jnp.zeros((count, LANES), jnp.float32)
        for k in range(k_sel):
            value = value + jnp.where(
                targets == tab[k : k + 1, :], tab[k_sel + k : k_sel + k + 1, :], 0.0
            )
        return value

    def spread(slot):
        own = table(slot, col * out_blocks, out_blocks)
        for at_lay in range(layers):
            for b in range(in_blocks):
                at = stride * at_lay + b
                splat_ref[at_lay, slot, b] = jnp.broadcast_to(
                    own[:, at : at + 1], (out_blocks, LANES)
                )

    edge = min(rows, TILE)
    folds = rows // edge
    across = LANES // edge
    metas, bases = [], {}

    def prepare(name, blocks):
        base = sum(-(-len(held) // across) for held, _, _ in bases.values())
        bases[name] = (blocks, base, len(metas))
        metas.extend(blocks)
        lane = lax.broadcasted_iota(jnp.int32, (out_blocks, LANES), 1) // edge
        same = lax.rem(lax.broadcasted_iota(jnp.int32, (edge, LANES), 1), edge) == (
            lax.broadcasted_iota(jnp.int32, (edge, LANES), 0)
        )
        for t in range(0, len(blocks), across):
            wide = jnp.zeros((out_blocks, LANES), jnp.float32)
            for i, (at_lay, slot, b) in enumerate(blocks[t : t + across]):
                wide = jnp.where(lane == i, splat_ref[at_lay, slot, b], wide)
            tile = base + t // across
            wide_ref[tile] = wide
            for o in range(out_blocks):
                mix_ref[tile, o * edge : (o + 1) * edge, :] = jnp.where(
                    same, jnp.broadcast_to(wide_ref[tile, o : o + 1, :], (edge, LANES)), 0.0
                ).astype(jnp.bfloat16)

    cut = out_blocks // CUTS
    cut_rows = [slice(low * edge, (low + cut) * edge) for low in range(0, out_blocks, cut)]

    def combine(name, source, sums):
        blocks, base, _ = bases[name]
        folded = jnp.concatenate(
            [
                source[:, h * edge : (h + 1) * edge, :].reshape(len(blocks) * edge, LANES)
                for h in range(folds)
            ],
            axis=1,
        )
        result = []
        for part, value in zip(cut_rows, sums):
            for t in range(0, len(blocks), across):
                width = min(across, len(blocks) - t) * edge
                term = jnp.dot(
                    mix_ref[base + t // across, part, :width],
                    folded[t * edge : t * edge + width],
                    preferred_element_type=jnp.float32,
                )
                value = term if value is None else value + term
            result.append(value)
        return result

    def put_sketch(sums):
        for i, value in enumerate(sums):
            value = (value + total_ref[cut_rows[i]]) * scale
            at = slice(cut * i * LANES, cut * (i + 1) * LANES)
            for h in range(folds):
                for r in range(0, edge, PUT):
                    sketch_ref[h * edge + r : h * edge + r + PUT, at] = jnp.concatenate(
                        [
                            value[o * edge + r : o * edge + r + PUT, h * LANES : (h + 1) * LANES]
                            for o in range(cut)
                        ],
                        axis=1,
                    ).astype(jnp.bfloat16)

    def await_wave(k):
        part = arrived_ref.at[wave_part(k)]
        to_sibling(part, part, send_sem.at[1], wave_sem.at[k]).wait_recv()

    def wave_blocks(k):
        first, count = waves[k]
        blocks = []
        for number in range(others):
            source = number + (chip <= number).astype(jnp.int32)
            for odd in range(2):
                slot = slot_of(2 * lax.rem(source, half) + odd)
                blocks += [(source // half, slot, first + b) for b in range(count)]
        return blocks

    def add_scores(name, source):
        blocks, values = bases[name][0], []
        for q in range(per_col):
            value = score_ref[q]
            for i, (at_lay, slot, b) in enumerate(blocks):
                value = value + source[i].astype(jnp.float32) * weights_ref[
                    slot, at_lay, b : b + 1, q * LANES : (q + 1) * LANES
                ]
            score_ref[q] = value
            values.append(value)
        return values

    def wave_values(k):
        first, count = waves[k]
        low = 2 * others * first
        return arrived_ref[low : low + 2 * others * count]

    spread(0)
    prepare("own", [(lay, 0, b) for b in range(in_blocks)])
    none = [None] * CUTS
    for part, value in zip(cut_rows, combine("own", owned_ref[lay], none)):
        total_ref[part] = value
    @pl.when(chip == others)
    def _():
        lax.fori_loop(1, others, send_pieces(range(len(waves))), 0)

    near = slot_of(sibling)

    odd_core = core == 1

    def take(k):
        await_wave(k)
        relay_copy(k).start()

    pl.when(chip > 0)(queries_up)

    all_tabs().wait_recv()
    for slot in range(1, n_col):
        spread(slot)
    prepare("sibling", [(lay, near, b) for b in range(in_blocks)])
    for k in range(len(waves)):
        prepare(k, wave_blocks(k))
    to_sibling(sibling_ref, sibling_ref, send_sem.at[0], sibling_sem.at[0]).wait_recv()
    for part, value in zip(cut_rows, combine("sibling", sibling_ref[...], none)):
        total_ref[part] = total_ref[part] + value
    for slot in range(n_col):
        whole = table(slot, 0, n_col * out_blocks).T
        for at_lay in range(layers):
            at = stride * at_lay
            turned_tab_ref[slot, at_lay] = whole[at : at + padded].astype(jnp.bfloat16)

    def put_scores(values):
        for q, value in enumerate(values):
            scores_ref[q : q + 1, :] = jnp.sum(value.T, axis=0, keepdims=True) * scale

    def start_scores():
        pltpu.make_async_copy(queries_ref, queries_ref, query_sem.at[1]).wait()
        asked = jnp.concatenate(
            [
                queries_ref[j * n_col : (j + 1) * n_col].reshape(n_col * out_blocks, LANES)
                for j in range(per_col)
            ],
            axis=1,
        )
        weights_ref[...] = jnp.dot(
            turned_tab_ref[...].reshape(n_col * layers * padded, n_col * out_blocks),
            asked,
            preferred_element_type=jnp.float32,
        ).reshape(weights_ref.shape)
        score_ref[...] = jnp.zeros_like(score_ref)
        add_scores("own", owned_ref[lay])
        add_scores("sibling", sibling_ref[...])

    timely = jnp.logical_or(
        asked_first == ex, jnp.logical_and(asked_first > ex, jnp.logical_not(odd_core))
    )

    @pl.when(jnp.logical_not(timely))
    def _():
        weights_ref[...] = jnp.zeros_like(weights_ref)
        score_ref[...] = jnp.zeros_like(score_ref)

    pl.when(jnp.logical_and(timely, jnp.logical_not(odd_core)))(start_scores)
    pl.when(chip == 0)(queries_up)
    last = len(waves) - 1
    sums = none
    for k in range(len(waves)):
        if k == 0:

            @pl.when(odd_core)
            def _():
                for later in range(len(waves)):
                    take(later)
                pl.when(timely)(start_scores)

        pl.when(jnp.logical_not(odd_core))(lambda: await_wave(k))
        if k == last:
            put_scores(add_scores(k, wave_values(k)))
        sums = combine(k, wave_values(k), sums)
        if k == last:
            put_sketch(sums)
        if k < last:
            add_scores(k, wave_values(k))

    @pl.when(jnp.logical_not(timely))
    def _():
        start_scores()
        for k in range(len(waves)):
            values = add_scores(k, wave_values(k))
        put_scores(values)

    part = arrived_ref.at[pl.ds(0, (others + 1) * in_blocks)]
    to_sibling(part, part, send_sem.at[0], wave_sem.at[0]).wait_send()
    all_tabs().wait_send()

    @pl.when(odd_core)
    def _():
        to_sibling(arrived_ref, arrived_ref, send_sem.at[1], wave_sem.at[0]).wait_send()

    def sent_queries(count):
        part = queries_ref.at[pl.ds(0, count)]
        to_sibling(part, part, query_sem.at[0], query_sem.at[1]).wait_send()

    pl.when(jnp.logical_not(mine))(lambda: sent_queries(n_ex))
    if n_ex > 1:
        pl.when(mine)(lambda: sent_queries(n_ex - 1))


def put_out(sketch_ref, scores_ref, sketch_hbm, scores_hbm, sem):
    for first in range(0, sketch_ref.shape[0], PUT):
        part = pl.ds(first, PUT)
        pltpu.make_async_copy(sketch_ref.at[part], sketch_hbm.at[part], sem.at[0]).start()
    scores = pltpu.make_async_copy(scores_ref, scores_hbm, sem.at[1])
    scores.start()
    pltpu.make_async_copy(sketch_ref, sketch_hbm, sem.at[0]).wait()
    scores.wait()


def solution(mesh):
    n_ex, n_col, n_lay = (mesh.shape[name] for name in ("ex", "col", "lay"))

    def local(normalized, upstream, owner_order, sketch_index, sketch_scale, query_sketch):
        examples, own_layers, tokens, features = normalized.shape
        layers, in_blocks, k_sel = sketch_index.shape
        width = query_sketch.shape[1]
        out_blocks = width // LANES
        assert TILE % tokens == 0 and examples * tokens % TILE == 0
        assert own_layers == 1 and query_sketch.shape[0] == 1 and n_col % 2 == 0
        assert n_col * out_blocks <= 256 and in_blocks <= LANES // layers
        per_col = n_ex // n_col
        rows = examples // n_lay
        waves = len(cuts(in_blocks))
        others = n_lay * n_col // 2 - 1
        edge = min(rows, TILE)
        padded = LANES // layers if in_blocks > TILE else TILE
        groups = [in_blocks] * 2 + [2 * others * count for _, count in cuts(in_blocks)]
        tiles = sum(-(-blocks * edge // LANES) for blocks in groups)
        vmem = pl.BlockSpec(memory_space=pltpu.VMEM)
        hbm = pl.BlockSpec(memory_space=pl.ANY)
        dma = pltpu.SemaphoreType.DMA
        sketch, scores = pl.pallas_call(
            functools.partial(kernel, (n_ex, n_col, n_lay, per_col, k_sel)),
            out_shape=(
                pltpu.VMEM((rows, width), jnp.bfloat16),
                pltpu.VMEM((per_col, rows), jnp.float32),
            ),
            in_specs=[hbm] * 6,
            out_specs=(vmem, vmem),
            scratch_shapes=[
                pltpu.VMEM(owner_order.shape, jnp.int32),
                pltpu.VMEM((layers, k_sel, in_blocks), jnp.int32),
                pltpu.VMEM((layers, k_sel, in_blocks), jnp.bfloat16),
                pltpu.VMEM(query_sketch.shape, jnp.bfloat16),
                pltpu.VMEM((2, examples * tokens // TILE, TILE, features), jnp.bfloat16),
                pltpu.VMEM((n_lay, in_blocks, rows, LANES), jnp.bfloat16),
                pltpu.VMEM((2 * others * in_blocks, rows, LANES), jnp.bfloat16),
                pltpu.VMEM((in_blocks, rows, LANES), jnp.bfloat16),
                pltpu.VMEM((2 * k_sel, LANES), jnp.float32),
                pltpu.VMEM((n_col, 2 * k_sel, LANES), jnp.bfloat16),
                pltpu.VMEM((out_blocks, LANES), jnp.float32),
                pltpu.VMEM((out_blocks, LANES), jnp.bfloat16),
                pltpu.VMEM((n_ex, out_blocks, LANES), jnp.bfloat16),
                pltpu.VMEM((LANES, LANES), jnp.bfloat16),
                pltpu.VMEM((layers, n_col, in_blocks, out_blocks, LANES), jnp.float32),
                pltpu.VMEM((n_col, layers, padded, n_col * out_blocks), jnp.bfloat16),
                pltpu.VMEM((n_col, layers, padded, per_col * LANES), jnp.float32),
                pltpu.VMEM((tiles, out_blocks, LANES), jnp.float32),
                pltpu.VMEM((tiles, out_blocks * edge, LANES), jnp.bfloat16),
                pltpu.VMEM((out_blocks * edge, rows // edge * LANES), jnp.float32),
                pltpu.VMEM((per_col, rows, LANES), jnp.float32),
                dma((min(waves, 2),)),
                dma((4,)),
                dma((2,)),
                dma((waves,)),
                dma((1,)),
                dma((2,)),
                dma((2,)),
                pltpu.SemaphoreType.REGULAR((2,)),
            ],
            compiler_params=pltpu.CompilerParams(collective_id=0, has_side_effects=True),
        )(
            normalized.reshape(examples, tokens, features),
            upstream.reshape(examples, tokens, features),
            owner_order,
            jnp.swapaxes(sketch_index, 1, 2),
            jnp.swapaxes(sketch_scale, 1, 2),
            query_sketch,
        )
        sketch, scores = pl.pallas_call(
            put_out,
            out_shape=(
                jax.ShapeDtypeStruct(sketch.shape, sketch.dtype),
                jax.ShapeDtypeStruct(scores.shape, scores.dtype),
            ),
            in_specs=[vmem, vmem],
            out_specs=(hbm, hbm),
            scratch_shapes=[dma((2,))],
            compiler_params=pltpu.CompilerParams(vmem_limit_bytes=1 << 20),
        )(sketch, scores)
        return sketch, scores.T

    placed = (
        P("ex", "lay", None, "col"),
        P("ex", "lay", None, "col"),
        P("ex", None),
        P(None, "col", None),
        P(None, "col", None),
        P("ex", "col"),
    )
    return jax.shard_map(
        local,
        mesh=mesh,
        in_specs=placed,
        out_specs=(P(("ex", "lay"), "col"), P(("ex", "lay"), "col")),
        check_vma=False,
    )
```

```python
import functools
import math

import jax
import jax.numpy as jnp
from jax import lax
from jax.experimental import pallas as pl
from jax.experimental.pallas import tpu as pltpu
from jax.sharding import PartitionSpec as P

MESH = pl.DeviceIdType.MESH
LANES = 128
WAVES = 4
TILE = 16
CUTS = 4
PUT = 8


def cuts(total):
    waves = min(WAVES, total)
    sizes = [total // waves + (i < total % waves) for i in range(waves)]
    return [(sum(sizes[:i]), sizes[i]) for i in range(waves)]


def batches(waves):
    heads = [(*waves[0], [0])]
    tail = waves[1:]
    if tail:
        heads.append((tail[0][0], sum(count for _, count in tail), list(range(1, len(waves)))))
    return heads


def signs():
    bits = lax.broadcasted_iota(jnp.int32, (LANES, LANES), 0) & lax.broadcasted_iota(
        jnp.int32, (LANES, LANES), 1
    )
    bits = bits ^ (bits >> 4)
    bits = bits ^ (bits >> 2)
    bits = bits ^ (bits >> 1)
    return (1 - 2 * (bits & 1)).astype(jnp.float32).astype(jnp.bfloat16)


def kernel(
    sizes,
    x_hbm,
    u_hbm,
    order_hbm,
    index_hbm,
    scale_hbm,
    query_hbm,
    sketch_ref,
    scores_ref,
    order_ref,
    index_ref,
    scale_ref,
    query_ref,
    xu_ref,
    owned_ref,
    arrived_ref,
    sibling_ref,
    own_tab_ref,
    tabs_ref,
    own_query_f32_ref,
    own_query_ref,
    queries_ref,
    had_ref,
    splat_ref,
    turned_tab_ref,
    weights_ref,
    wide_ref,
    mix_ref,
    total_ref,
    score_ref,
    load_sem,
    small_sem,
    send_sem,
    wave_sem,
    sibling_sem,
    tab_sem,
    query_sem,
    ready_sem,
):
    n_ex, n_col, n_lay, per_col, k_sel = sizes
    ex, col, lay = lax.axis_index("ex"), lax.axis_index("col"), lax.axis_index("lay")
    examples, tokens, features = x_hbm.shape
    pack = TILE // tokens
    rows = examples // n_lay
    in_blocks = features // LANES
    layers = index_ref.shape[0]
    stride = LANES // layers
    padded = weights_ref.shape[2]
    out_blocks = query_ref.shape[1] // LANES
    half = n_col // 2
    others = n_lay * half - 1
    core, chip = lax.rem(col, 2), lay * half + col // 2
    sibling = col + 1 - 2 * core
    scale = 1.0 / math.sqrt(float(LANES))
    waves = cuts(in_blocks)

    barrier = pltpu.get_barrier_semaphore()
    asker = ex // per_col
    asked_first = col * per_col

    def greet(sem, at_ex, at_col, at_lay):
        pl.semaphore_signal(
            sem,
            inc=1,
            device_id={"ex": at_ex, "col": at_col, "lay": at_lay},
            device_id_type=MESH,
        )

    def greet_chip(sem, target):
        for odd in range(2):
            greet(sem, ex, 2 * lax.rem(target, half) + odd, target // half)

    def greet_chips(sem, start, stop):
        def body(target, carry):
            greet_chip(sem, target)
            return carry

        lax.fori_loop(start, stop, body, 0)

    def greet_askers(at_ex, carry):
        greet(barrier, at_ex, asker, lay)
        return carry

    def greet_sources(sem):
        def body(at_ex, carry):
            for at_col in range(n_col):
                greet(sem, at_ex, at_col, lay)
            return carry

        return body

    below = jnp.clip(ex - asked_first, 0, per_col)
    greeted = jnp.where(chip == others, others, jnp.minimum(chip, 1))
    greetings = 1 + 2 * greeted + ex + n_col * below

    def known(target):
        return jnp.logical_or(
            target == chip, jnp.logical_or(chip == others, jnp.logical_and(target == 0, chip > 0))
        )

    parts = batches(waves)
    load_parts = [pl.ds(first * LANES, count * LANES) for first, count, _ in parts]
    smalls = [
        pltpu.make_async_copy(source, held, small_sem.at[i])
        for i, (source, held) in enumerate(
            [
                (order_hbm, order_ref),
                (index_hbm, index_ref),
                (scale_hbm, scale_ref),
                (query_hbm, query_ref),
            ]
        )
    ]
    for copy in smalls:
        copy.start()
    for k, part in enumerate(load_parts):
        for i, source in enumerate((x_hbm, u_hbm)):
            tiles = examples // pack
            split = source.reshape(tiles, pack, tokens, features)
            step = tiles // 4 if k and tiles % 4 == 0 else tiles
            for low in range(0, tiles, step):
                for r in range(pack):
                    pltpu.make_async_copy(
                        split.at[pl.ds(low, step), r, :, part],
                        xu_ref.at[i, pl.ds(low, step), pl.ds(r * tokens, tokens), part],
                        load_sem.at[k],
                    ).start()

    pl.when(chip == 0)(lambda: greet_chips(barrier, 1, others + 1))
    pl.when(jnp.logical_and(chip > 0, chip < others))(lambda: greet_chip(barrier, others))
    greet(barrier, ex, sibling, lay)
    lax.fori_loop(ex + 1, n_ex, greet_askers, 0)
    lax.fori_loop(
        jnp.maximum(ex + 1, asked_first), asked_first + per_col, greet_sources(barrier), 0
    )
    pl.semaphore_wait(barrier, greetings)
    pl.when(jnp.logical_and(chip > 0, chip < others))(lambda: greet_chip(ready_sem.at[1], 0))
    pl.when(chip == others)(lambda: greet_chips(ready_sem.at[1], 0, others))
    lax.fori_loop(
        asked_first, jnp.minimum(asked_first + per_col, ex), greet_sources(ready_sem.at[0]), 0
    )

    had_ref[...] = signs()
    own_tab_ref[...] = jnp.full(own_tab_ref.shape, -1.0, jnp.float32)

    def turn(stacked):
        return jnp.dot(stacked, had_ref[...], preferred_element_type=jnp.float32)

    def wave_part(k):
        first, count = waves[k]
        return pl.ds(2 * others * first, 2 * others * count)

    def piece_copy(k, number):
        first, count = waves[k]
        target = number + (chip <= number).astype(jnp.int32)
        slot = chip - (chip > target).astype(jnp.int32)
        to_lay = target // half
        return pltpu.make_async_remote_copy(
            src_ref=owned_ref.at[to_lay, pl.ds(first, count)],
            dst_ref=arrived_ref.at[
                pl.ds(2 * others * first + (2 * slot + core) * count, count)
            ],
            send_sem=send_sem.at[0],
            recv_sem=wave_sem.at[k],
            device_id={"ex": ex, "col": 2 * lax.rem(target, half) + 1, "lay": to_lay},
            device_id_type=MESH,
        )

    def to_sibling(source, target, send, recv):
        return pltpu.make_async_remote_copy(
            src_ref=source,
            dst_ref=target,
            send_sem=send,
            recv_sem=recv,
            device_id={"ex": ex, "col": sibling, "lay": lay},
            device_id_type=MESH,
        )

    def own_copy(first, count):
        part = pl.ds(first, count)
        return to_sibling(
            owned_ref.at[lay, part], sibling_ref.at[part], send_sem.at[0], sibling_sem.at[0]
        )

    def relay_copy(k):
        part = arrived_ref.at[wave_part(k)]
        return to_sibling(part, part, send_sem.at[1], wave_sem.at[k])

    def tab_copy(dc):
        return pltpu.make_async_remote_copy(
            src_ref=tabs_ref.at[0],
            dst_ref=tabs_ref.at[dc],
            send_sem=tab_sem.at[0],
            recv_sem=tab_sem.at[1],
            device_id={"ex": ex, "col": lax.rem(col + dc, n_col), "lay": lay},
            device_id_type=MESH,
        )

    def all_tabs():
        part = tabs_ref.at[pl.ds(1, n_col - 1)]
        return to_sibling(part, part, tab_sem.at[0], tab_sem.at[1])

    smalls[0].wait()
    chosen = (
        lax.broadcasted_iota(jnp.int32, (examples * tokens, examples), 0) // tokens
        == order_ref[...]
    ).astype(jnp.float32)
    chosen = chosen.T.astype(jnp.bfloat16)

    def make(k):
        first, count, _ = parts[k]
        part = load_parts[k]
        pltpu.make_async_copy(
            xu_ref.at[:, :, :, part], xu_ref.at[:, :, :, part], load_sem.at[k]
        ).wait()
        ordered = []
        for b in range(first, first + count):
            x, u = (
                xu_ref[i, :, :, b * LANES : (b + 1) * LANES]
                .reshape(examples * tokens, LANES)
                .astype(jnp.float32)
                for i in range(2)
            )
            product = x * u
            high = product.astype(jnp.bfloat16)
            low = (product - high.astype(jnp.float32)).astype(jnp.bfloat16)
            ordered.append(
                (
                    jnp.dot(chosen, high, preferred_element_type=jnp.float32)
                    + jnp.dot(chosen, low, preferred_element_type=jnp.float32)
                ).astype(jnp.bfloat16)
            )
        for b in range(count):
            stacked = turn(ordered[b]).astype(jnp.bfloat16)
            for owner in range(n_lay):
                owned_ref[owner, first + b] = stacked[owner * rows : (owner + 1) * rows]

    place = lax.rem(ex, per_col) * n_col + col
    mine = asker == col

    def query_copy(target):
        return pltpu.make_async_remote_copy(
            src_ref=own_query_ref,
            dst_ref=queries_ref.at[place],
            send_sem=query_sem.at[0],
            recv_sem=query_sem.at[1],
            device_id={"ex": target, "col": asker, "lay": lay},
            device_id_type=MESH,
        )

    def send_query(target, carry):
        query_copy(target).start()
        return carry

    def send_pieces(ks):
        def body(number, carry):
            for k in ks:
                piece_copy(k, number).start()
            return carry

        return body

    def send_first(k):
        @pl.when(chip > 0)
        def _():
            for wave in parts[k][2]:
                piece_copy(wave, 0).start()

        own_copy(*parts[k][:2]).start()

    def tabs_to(greeted):
        for dc in range(1, n_col):
            target = lay * half + lax.rem(col + dc, n_col) // 2
            pl.when(known(target) == greeted)(lambda: tab_copy(dc).start())

    for copy in smalls[1:]:
        copy.wait()
    for layer in range(layers):
        at = slice(stride * layer, stride * layer + in_blocks)
        own_tab_ref[0:k_sel, at] = index_ref[layer].astype(jnp.float32)
        own_tab_ref[k_sel : 2 * k_sel, at] = scale_ref[layer].astype(jnp.float32)
    tabs_ref[0] = own_tab_ref[...].astype(jnp.bfloat16)
    for o in range(out_blocks):
        own_query_f32_ref[o : o + 1, :] = query_ref[:, o * LANES : (o + 1) * LANES].astype(
            jnp.float32
        )
    own_query_ref[...] = own_query_f32_ref[...].astype(jnp.bfloat16)
    tabs_to(True)
    def share_query():
        query_copy(ex).start()

    here = known(lay * half + asker // 2)

    @pl.when(mine)
    def _():
        pltpu.make_async_copy(own_query_ref, queries_ref.at[place], query_sem.at[1]).start()

    pl.when(jnp.logical_and(here, jnp.logical_not(mine)))(share_query)

    make(0)
    send_first(0)
    for k in range(1, len(parts)):
        make(k)
        send_first(k)


    @pl.when(chip < others)
    def _():
        pl.semaphore_wait(ready_sem.at[1], jnp.where(chip == 0, 2 * others, 2))
        tabs_to(False)
        pl.when(jnp.logical_not(here))(share_query)

        lax.fori_loop(jnp.minimum(chip, 1), others, send_pieces(range(len(waves))), 0)

    lax.fori_loop(0, ex, send_query, 0)

    def queries_up():
        @pl.when(ex < n_ex - 1)
        def _():
            pl.semaphore_wait(ready_sem.at[0], n_ex - 1 - ex)
            lax.fori_loop(ex + 1, n_ex, send_query, 0)

    def slot_of(source):
        return lax.rem(col - source + n_col, n_col)

    def table(slot, first, count):
        tab = tabs_ref[slot].astype(jnp.float32)
        targets = (first + lax.broadcasted_iota(jnp.int32, (count, LANES), 0)).astype(jnp.float32)
        value = jnp.zeros((count, LANES), jnp.float32)
        for k in range(k_sel):
            value = value + jnp.where(
                targets == tab[k : k + 1, :], tab[k_sel + k : k_sel + k + 1, :], 0.0
            )
        return value

    def spread(slot):
        own = table(slot, col * out_blocks, out_blocks)
        for at_lay in range(layers):
            for b in range(in_blocks):
                at = stride * at_lay + b
                splat_ref[at_lay, slot, b] = jnp.broadcast_to(
                    own[:, at : at + 1], (out_blocks, LANES)
                )

    edge = min(rows, TILE)
    folds = rows // edge
    across = LANES // edge
    metas, bases = [], {}

    def prepare(name, blocks):
        base = sum(-(-len(held) // across) for held, _, _ in bases.values())
        bases[name] = (blocks, base, len(metas))
        metas.extend(blocks)
        lane = lax.broadcasted_iota(jnp.int32, (out_blocks, LANES), 1) // edge
        same = lax.rem(lax.broadcasted_iota(jnp.int32, (edge, LANES), 1), edge) == (
            lax.broadcasted_iota(jnp.int32, (edge, LANES), 0)
        )
        for t in range(0, len(blocks), across):
            wide = jnp.zeros((out_blocks, LANES), jnp.float32)
            for i, (at_lay, slot, b) in enumerate(blocks[t : t + across]):
                wide = jnp.where(lane == i, splat_ref[at_lay, slot, b], wide)
            tile = base + t // across
            wide_ref[tile] = wide
            for o in range(out_blocks):
                mix_ref[tile, o * edge : (o + 1) * edge, :] = jnp.where(
                    same, jnp.broadcast_to(wide_ref[tile, o : o + 1, :], (edge, LANES)), 0.0
                ).astype(jnp.bfloat16)

    cut = out_blocks // CUTS
    cut_rows = [slice(low * edge, (low + cut) * edge) for low in range(0, out_blocks, cut)]

    def combine(name, source, sums):
        blocks, base, _ = bases[name]
        folded = jnp.concatenate(
            [
                source[:, h * edge : (h + 1) * edge, :].reshape(len(blocks) * edge, LANES)
                for h in range(folds)
            ],
            axis=1,
        )
        result = []
        for part, value in zip(cut_rows, sums):
            for t in range(0, len(blocks), across):
                width = min(across, len(blocks) - t) * edge
                term = jnp.dot(
                    mix_ref[base + t // across, part, :width],
                    folded[t * edge : t * edge + width],
                    preferred_element_type=jnp.float32,
                )
                value = term if value is None else value + term
            result.append(value)
        return result

    def put_sketch(sums):
        for i, value in enumerate(sums):
            value = (value + total_ref[cut_rows[i]]) * scale
            at = slice(cut * i * LANES, cut * (i + 1) * LANES)
            for h in range(folds):
                for r in range(0, edge, PUT):
                    sketch_ref[h * edge + r : h * edge + r + PUT, at] = jnp.concatenate(
                        [
                            value[o * edge + r : o * edge + r + PUT, h * LANES : (h + 1) * LANES]
                            for o in range(cut)
                        ],
                        axis=1,
                    ).astype(jnp.bfloat16)

    def await_wave(k):
        part = arrived_ref.at[wave_part(k)]
        to_sibling(part, part, send_sem.at[1], wave_sem.at[k]).wait_recv()

    def wave_blocks(k):
        first, count = waves[k]
        blocks = []
        for number in range(others):
            source = number + (chip <= number).astype(jnp.int32)
            for odd in range(2):
                slot = slot_of(2 * lax.rem(source, half) + odd)
                blocks += [(source // half, slot, first + b) for b in range(count)]
        return blocks

    def add_scores(name, source):
        blocks, values = bases[name][0], []
        for q in range(per_col):
            value = score_ref[q]
            for i, (at_lay, slot, b) in enumerate(blocks):
                value = value + source[i].astype(jnp.float32) * weights_ref[
                    slot, at_lay, b : b + 1, q * LANES : (q + 1) * LANES
                ]
            score_ref[q] = value
            values.append(value)
        return values

    def wave_values(k):
        first, count = waves[k]
        low = 2 * others * first
        return arrived_ref[low : low + 2 * others * count]

    spread(0)
    prepare("own", [(lay, 0, b) for b in range(in_blocks)])
    none = [None] * CUTS
    for part, value in zip(cut_rows, combine("own", owned_ref[lay], none)):
        total_ref[part] = value
    @pl.when(chip == others)
    def _():
        lax.fori_loop(1, others, send_pieces(range(len(waves))), 0)

    near = slot_of(sibling)

    odd_core = core == 1

    def take(k):
        await_wave(k)
        relay_copy(k).start()

    pl.when(chip > 0)(queries_up)

    all_tabs().wait_recv()
    for slot in range(1, n_col):
        spread(slot)
    prepare("sibling", [(lay, near, b) for b in range(in_blocks)])
    for k in range(len(waves)):
        prepare(k, wave_blocks(k))
    to_sibling(sibling_ref, sibling_ref, send_sem.at[0], sibling_sem.at[0]).wait_recv()
    for part, value in zip(cut_rows, combine("sibling", sibling_ref[...], none)):
        total_ref[part] = total_ref[part] + value
    for slot in range(n_col):
        whole = table(slot, 0, n_col * out_blocks).T
        for at_lay in range(layers):
            at = stride * at_lay
            turned_tab_ref[slot, at_lay] = whole[at : at + padded].astype(jnp.bfloat16)

    def put_scores(values):
        for q, value in enumerate(values):
            scores_ref[q : q + 1, :] = jnp.sum(value.T, axis=0, keepdims=True) * scale

    def start_scores():
        pltpu.make_async_copy(queries_ref, queries_ref, query_sem.at[1]).wait()
        asked = jnp.concatenate(
            [
                queries_ref[j * n_col : (j + 1) * n_col].reshape(n_col * out_blocks, LANES)
                for j in range(per_col)
            ],
            axis=1,
        )
        weights_ref[...] = jnp.dot(
            turned_tab_ref[...].reshape(n_col * layers * padded, n_col * out_blocks),
            asked,
            preferred_element_type=jnp.float32,
        ).reshape(weights_ref.shape)
        score_ref[...] = jnp.zeros_like(score_ref)
        add_scores("own", owned_ref[lay])
        add_scores("sibling", sibling_ref[...])

    timely = jnp.logical_or(
        asked_first == ex, jnp.logical_and(asked_first > ex, jnp.logical_not(odd_core))
    )

    @pl.when(jnp.logical_not(timely))
    def _():
        weights_ref[...] = jnp.zeros_like(weights_ref)
        score_ref[...] = jnp.zeros_like(score_ref)

    pl.when(jnp.logical_and(timely, jnp.logical_not(odd_core)))(start_scores)
    pl.when(chip == 0)(queries_up)
    last = len(waves) - 1
    sums = none
    for k in range(len(waves)):
        if k == 0:

            @pl.when(odd_core)
            def _():
                for later in range(len(waves)):
                    take(later)
                pl.when(timely)(start_scores)

        pl.when(jnp.logical_not(odd_core))(lambda: await_wave(k))
        if k == last:
            put_scores(add_scores(k, wave_values(k)))
        sums = combine(k, wave_values(k), sums)
        if k == last:
            put_sketch(sums)
        if k < last:
            add_scores(k, wave_values(k))

    @pl.when(jnp.logical_not(timely))
    def _():
        start_scores()
        for k in range(len(waves)):
            values = add_scores(k, wave_values(k))
        put_scores(values)

    part = arrived_ref.at[pl.ds(0, (others + 1) * in_blocks)]
    to_sibling(part, part, send_sem.at[0], wave_sem.at[0]).wait_send()
    all_tabs().wait_send()

    @pl.when(odd_core)
    def _():
        to_sibling(arrived_ref, arrived_ref, send_sem.at[1], wave_sem.at[0]).wait_send()

    def sent_queries(count):
        part = queries_ref.at[pl.ds(0, count)]
        to_sibling(part, part, query_sem.at[0], query_sem.at[1]).wait_send()

    pl.when(jnp.logical_not(mine))(lambda: sent_queries(n_ex))
    if n_ex > 1:
        pl.when(mine)(lambda: sent_queries(n_ex - 1))


def put_out(sketch_ref, scores_ref, sketch_hbm, scores_hbm, sem):
    for first in range(0, sketch_ref.shape[0], PUT):
        part = pl.ds(first, PUT)
        pltpu.make_async_copy(sketch_ref.at[part], sketch_hbm.at[part], sem.at[0]).start()
    scores = pltpu.make_async_copy(scores_ref, scores_hbm, sem.at[1])
    scores.start()
    pltpu.make_async_copy(sketch_ref, sketch_hbm, sem.at[0]).wait()
    scores.wait()


def solution(mesh):
    n_ex, n_col, n_lay = (mesh.shape[name] for name in ("ex", "col", "lay"))

    def local(normalized, upstream, owner_order, sketch_index, sketch_scale, query_sketch):
        examples, own_layers, tokens, features = normalized.shape
        layers, in_blocks, k_sel = sketch_index.shape
        width = query_sketch.shape[1]
        out_blocks = width // LANES
        assert TILE % tokens == 0 and examples * tokens % TILE == 0
        assert own_layers == 1 and query_sketch.shape[0] == 1 and n_col % 2 == 0
        assert n_col * out_blocks <= 256 and in_blocks <= LANES // layers
        per_col = n_ex // n_col
        rows = examples // n_lay
        waves = len(cuts(in_blocks))
        others = n_lay * n_col // 2 - 1
        edge = min(rows, TILE)
        padded = LANES // layers if in_blocks > TILE else TILE
        groups = [in_blocks] * 2 + [2 * others * count for _, count in cuts(in_blocks)]
        tiles = sum(-(-blocks * edge // LANES) for blocks in groups)
        vmem = pl.BlockSpec(memory_space=pltpu.VMEM)
        hbm = pl.BlockSpec(memory_space=pl.ANY)
        dma = pltpu.SemaphoreType.DMA
        sketch, scores = pl.pallas_call(
            functools.partial(kernel, (n_ex, n_col, n_lay, per_col, k_sel)),
            out_shape=(
                pltpu.VMEM((rows, width), jnp.bfloat16),
                pltpu.VMEM((per_col, rows), jnp.float32),
            ),
            in_specs=[hbm] * 6,
            out_specs=(vmem, vmem),
            scratch_shapes=[
                pltpu.VMEM(owner_order.shape, jnp.int32),
                pltpu.VMEM((layers, k_sel, in_blocks), jnp.int32),
                pltpu.VMEM((layers, k_sel, in_blocks), jnp.bfloat16),
                pltpu.VMEM(query_sketch.shape, jnp.bfloat16),
                pltpu.VMEM((2, examples * tokens // TILE, TILE, features), jnp.bfloat16),
                pltpu.VMEM((n_lay, in_blocks, rows, LANES), jnp.bfloat16),
                pltpu.VMEM((2 * others * in_blocks, rows, LANES), jnp.bfloat16),
                pltpu.VMEM((in_blocks, rows, LANES), jnp.bfloat16),
                pltpu.VMEM((2 * k_sel, LANES), jnp.float32),
                pltpu.VMEM((n_col, 2 * k_sel, LANES), jnp.bfloat16),
                pltpu.VMEM((out_blocks, LANES), jnp.float32),
                pltpu.VMEM((out_blocks, LANES), jnp.bfloat16),
                pltpu.VMEM((n_ex, out_blocks, LANES), jnp.bfloat16),
                pltpu.VMEM((LANES, LANES), jnp.bfloat16),
                pltpu.VMEM((layers, n_col, in_blocks, out_blocks, LANES), jnp.float32),
                pltpu.VMEM((n_col, layers, padded, n_col * out_blocks), jnp.bfloat16),
                pltpu.VMEM((n_col, layers, padded, per_col * LANES), jnp.float32),
                pltpu.VMEM((tiles, out_blocks, LANES), jnp.float32),
                pltpu.VMEM((tiles, out_blocks * edge, LANES), jnp.bfloat16),
                pltpu.VMEM((out_blocks * edge, rows // edge * LANES), jnp.float32),
                pltpu.VMEM((per_col, rows, LANES), jnp.float32),
                dma((min(waves, 2),)),
                dma((4,)),
                dma((2,)),
                dma((waves,)),
                dma((1,)),
                dma((2,)),
                dma((2,)),
                pltpu.SemaphoreType.REGULAR((2,)),
            ],
            compiler_params=pltpu.CompilerParams(collective_id=0, has_side_effects=True),
        )(
            normalized.reshape(examples, tokens, features),
            upstream.reshape(examples, tokens, features),
            owner_order,
            jnp.swapaxes(sketch_index, 1, 2),
            jnp.swapaxes(sketch_scale, 1, 2),
            query_sketch,
        )
        sketch, scores = pl.pallas_call(
            put_out,
            out_shape=(
                jax.ShapeDtypeStruct(sketch.shape, sketch.dtype),
                jax.ShapeDtypeStruct(scores.shape, scores.dtype),
            ),
            in_specs=[vmem, vmem],
            out_specs=(hbm, hbm),
            scratch_shapes=[dma((2,))],
            compiler_params=pltpu.CompilerParams(vmem_limit_bytes=1 << 20),
        )(sketch, scores)
        return sketch, scores.T

    placed = (
        P("ex", "lay", None, "col"),
        P("ex", "lay", None, "col"),
        P("ex", None),
        P(None, "col", None),
        P(None, "col", None),
        P("ex", "col"),
    )
    return jax.shard_map(
        local,
        mesh=mesh,
        in_specs=placed,
        out_specs=(P(("ex", "lay"), "col"), P(("ex", "lay"), "col")),
        check_vma=False,
    )
```
